32 devices in a mesh: groups: 2 (over x), agent: 8 (over z, y), tm: 2 (over core).
Axes of the slice: x: 2, y: 2, z: 4, core: 2. Of those that a mesh axis runs over, the one named last changes fastest.
Arguments:
- embedded: bfloat16 [64, 1024, 512], P(('groups', 'tm'), 'agent'), parts along dimension 0, may hold values from -6 to 6
- block_lists: int32 [16, 32, 2], P(('groups', 'agent'), 'tm'), parts along dimension 0, may hold values from 0 to 7, all different within a row; in each aligned block of 16 rows (0 to 15, 16 to 31, ..., all dimensions but the last counted through in order) at most 8 rows name the same one
- done_flags: int32 [64, 1024], P(('groups', 'tm'), 'agent'), parts along dimension 0, may hold values 0 or 1
- rewards: float32 [64, 1024], P(('groups', 'tm'), 'agent'), parts along dimension 0, may hold values from -1.2 to 1.2
- bootstrap: float32 [2048], P(('groups', 'agent')), parts along dimension 0, may hold values from -6 to 6
- agent_proj: bfloat16 [512, 1536], replicated, may hold values from -2 to 2
- agent_merge: bfloat16 [512, 512], replicated, may hold values from -0.75 to 0.75
- time_proj: bfloat16 [512, 1536], replicated, may hold values from -2 to 2
- time_merge: bfloat16 [512, 512], replicated, may hold values from -0.75 to 0.75
- value_weight: float32 [512], replicated, may hold values from -0.25 to 0.25
Outputs:
- values: float32 [64, 1024], P(('groups', 'tm'), 'agent'), parts along dimension 0
- advantages: float32 [64, 1024], P(('groups', 'tm'), 'agent'), parts along dimension 0
The draws below stay inside these ranges and needn't reach their ends.
There are 2 independent parts, one for each index of `groups`. The reference program is written for one: setup_inputs(seed, part) draws one part's arguments, and reference() takes and returns one part's arrays. A program takes and returns all parts, laid end to end along the dimension named above; an argument that names none is the same for every part. Nothing has to cross between parts.
Inputs may be any that keep to these rules, and one draw needn't show every extreme that they name: `block_lists`: each row names 2 different agent blocks. Within the 16 rows of one block along the second dimension no agent block is named more than 8 times, and some agent block is named exactly 8 times.
All inputs are finite; a program needn't handle non-finite values. No bound on the sum of `done_flags` on one device may be relied on, other than what follows from the above.
Results may differ from the reference program's by a relative error of at most 0.0085.
Values may be sent and summed in bfloat16 or wider, within the bound.
A program may use at most 128 MiB of HBM per device.

```python
import math
import jax
import jax.numpy as jnp
import numpy as np
from jax import lax

D = 512
HEADS = 8
HEAD = 64
AGT_DEV = 128
STEPS_DEV = 16
WINDOW = 16
LIST = 2
CAP = 8
BLOCKS = 8
AGENTS = 1024
STEPS = 32


def projection_draw(key):
    queries = jax.random.normal(jax.random.fold_in(key, 11), (D, HEADS, HEAD), jnp.float32) * D ** (-0.5)
    keys_part = jax.random.normal(jax.random.fold_in(key, 12), (D, HEADS, HEAD), jnp.float32) * D ** (-0.5)
    values_part = jax.random.normal(jax.random.fold_in(key, 13), (D, HEADS, HEAD), jnp.float32) * D ** (-0.5)
    stacked = jnp.stack([queries, keys_part, values_part], axis=1)
    stacked = jnp.clip(stacked, -2.0, 2.0)
    return stacked.reshape(D, 3 * D).astype(jnp.bfloat16)


def draw_agent_proj(key, part):
    return projection_draw(jax.random.fold_in(key, 1))


def draw_time_proj(key, part):
    return projection_draw(jax.random.fold_in(key, 2))


def set_ends(values, own_key, smallest, largest):
    longest = values.shape.index(max(values.shape))
    spots = []
    for shift in (0, 1):
        where = [jax.random.randint(jax.random.fold_in(own_key, axis), (), 0, length) for axis, length in enumerate(values.shape)]
        where[longest] = (where[longest] + shift) % values.shape[longest]
        spots.append(tuple(where))
    return values.at[spots[0]].set(smallest).at[spots[1]].set(largest)


def block_scale(rng, shape, split, least, high):
    def one(position, shards_of):
        draws = jax.random.uniform(jax.random.fold_in(jax.random.fold_in(rng, 6), position), (shards_of,), jnp.float32, least / len(split), high / len(split))
        return jnp.repeat(jnp.exp(draws), shape[position] // shards_of).reshape((-1,) + (1,) * (len(shape) - position - 1))

    gain = one(*split[0])
    for cut in split[1:]:
        gain = gain * one(*cut)
    return gain


def assign_block(rng, own, number, rows, amount, top, limit, slope):
    ranking = jax.random.permutation(rng, amount)
    crowded, ordinary = load_shares(amount, rows * top, limit, slope, True), load_shares(amount, rows * top, limit, slope, False)
    places = jnp.arange(amount)

    def named(sizes, offset_by):
        used = int((sizes > 0).sum())
        fixed = max(1, used // 4)
        moved = fixed + (places - fixed + offset_by * (used - fixed)) % max(1, amount - fixed)
        return jnp.zeros((amount,), jnp.int32).at[ranking[jnp.where(places < fixed, places, moved)]].set(jnp.asarray(sizes, jnp.int32))

    sizes = jnp.where(number % 4 == 0, named(crowded, number // 4), named(ordinary, number - number // 4 - 1))
    mixed = jax.random.permutation(jax.random.fold_in(own, 3), amount)
    donor, receiver = mixed[0:amount // 2 * 2:2], mixed[1:amount // 2 * 2:2]
    room = jnp.minimum(sizes[donor] - 1, limit - sizes[receiver]) // 2
    room = jnp.where((donor == ranking[0]) | (receiver == ranking[0]) | (sizes[receiver] == 0), 0, jnp.maximum(room, 0))
    moved = jax.random.randint(jax.random.fold_in(own, 4), (amount // 2,), 0, 1 << 20) % (room + 1)
    sizes = sizes.at[donor].add(-moved).at[receiver].add(moved)
    items = jnp.searchsorted(jnp.cumsum(sizes), jnp.arange(rows * top), side="right").astype(jnp.int32)
    listing = items.reshape(top, rows).T
    listing = listing[jax.random.permutation(jax.random.fold_in(own, 1), rows)]
    offset_by = jax.random.randint(jax.random.fold_in(own, 2), (rows, 1), 0, top)
    return jnp.take_along_axis(listing, (jnp.arange(top)[None, :] + offset_by) % top, axis=1)


def load_shares(amount, total, reach, skew, full):
    portions = [(1 << 20) // math.isqrt(grade ** skew) + 1 for grade in range(1, amount + 1)]
    largest = reach if full else min(reach, max(-(-total // amount), total * portions[0] // sum(portions)))
    least = 1 if total - largest >= amount - 1 else 0
    holding, surplus = [largest] + [least] * (amount - 1), total - largest - least * (amount - 1)
    while surplus > 0:
        movable = [i for i in range(1, amount) if holding[i] < largest] or [i for i in range(1, amount) if holding[i] < reach]
        pool, remaining = sum([portions[i] for i in movable]), surplus
        for i in movable:
            addition = min(reach - holding[i], max(1, remaining * portions[i] // pool), surplus)
            holding[i] = holding[i] + addition
            surplus = surplus - addition
    return np.array(holding)


def normal_values(rng, shape, spread, most, split=(), kind=jnp.bfloat16):
    values = spread * jax.random.normal(rng, shape, jnp.float32)
    if split:
        values = values * block_scale(rng, shape, split, -0.22, 0.18)
    return jnp.clip(values, -most, most).astype(kind)


def setup_inputs(seed: int = 0, part: int = 0) -> dict:
    splits = jax.random.split(jax.random.key(seed), 11)
    part_keys = jax.random.split(jax.random.fold_in(splits[10], part), 11)
    embedded = normal_values(part_keys[0], (STEPS, AGENTS, D), 1.0, 6.0, ((0, 2), (1, 8)))
    block_lists_keys = jax.random.split(jax.random.fold_in(part_keys[1], 1), BLOCKS * STEPS // STEPS_DEV)
    block_lists_turns = jax.random.permutation(jax.random.fold_in(part_keys[1], 3), BLOCKS * STEPS // STEPS_DEV)
    block_lists = jax.vmap(lambda own, number: assign_block(jax.random.fold_in(part_keys[1], 2), own, number, STEPS_DEV, BLOCKS, LIST, CAP, 2))(block_lists_keys, block_lists_turns).reshape((BLOCKS, STEPS, LIST))
    done_flags = set_ends((jax.random.randint(part_keys[2], (STEPS, AGENTS), 0, 32) < 1).astype(jnp.int32), jax.random.fold_in(part_keys[2], 1), 0, 1)
    rewards = normal_values(part_keys[3], (STEPS, AGENTS), 0.2, 1.2, ((0, 2), (1, 8)), jnp.float32)
    bootstrap = normal_values(part_keys[4], (AGENTS,), 1.0, 6.0, ((0, 8),), jnp.float32)
    agent_proj = draw_agent_proj(jax.random.fold_in(splits[10], 71), part)
    agent_merge = normal_values(splits[6], (D, D), HEAD ** -0.5, 0.75)
    time_proj = draw_time_proj(jax.random.fold_in(splits[10], 71), part)
    time_merge = normal_values(splits[8], (D, D), HEAD ** -0.5, 0.75)
    value_weight = normal_values(splits[9], (D,), D ** -0.5, 0.25, (), jnp.float32)
    return {"embedded": embedded, "block_lists": block_lists, "done_flags": done_flags, "rewards": rewards, "bootstrap": bootstrap, "agent_proj": agent_proj, "agent_merge": agent_merge, "time_proj": time_proj, "time_merge": time_merge, "value_weight": value_weight}


discount = 0.9997
trace_decay = 0.995
epsilon = 1e-06

def rms_norm(values):
    return values * lax.rsqrt(lax.optimization_barrier(jnp.mean(values * values, axis=-1, keepdims=True)) + epsilon)

def softmax_rows(scores):
    shifted = scores - lax.optimization_barrier(jnp.max(scores, axis=-1, keepdims=True))
    exponent = jnp.exp(shifted)
    return exponent / lax.optimization_barrier(jnp.sum(exponent, axis=-1, keepdims=True))

def reference(embedded, block_lists, done_flags, rewards, bootstrap, agent_proj, agent_merge, time_proj, time_merge, value_weight):
    tokens = STEPS * AGENTS
    score_scale = HEAD ** (-0.5)
    residual = embedded.astype(jnp.float32).reshape(tokens, D)
    normed = rms_norm(residual).astype(jnp.bfloat16)
    projected = jnp.dot(normed, agent_proj, preferred_element_type=jnp.float32).astype(jnp.bfloat16)
    projected = projected.reshape(STEPS, BLOCKS, AGT_DEV, 3, HEADS, HEAD)

    def agent_step(step):
        step_rows = projected[step]
        listed = step_rows[block_lists[:, step, :]]
        all_keys = jnp.concatenate([step_rows[:, None], listed], axis=1)
        all_keys = all_keys.reshape(BLOCKS, (1 + LIST) * AGT_DEV, 3, HEADS, HEAD)
        queries = step_rows[:, :, 0].astype(jnp.float32)
        scores = jnp.einsum('bqhe,bkhe->bhqk', queries, all_keys[:, :, 1].astype(jnp.float32)) * score_scale
        attention = softmax_rows(scores).astype(jnp.bfloat16)
        attended = jnp.einsum('bhqk,bkhe->bqhe', attention.astype(jnp.float32), all_keys[:, :, 2].astype(jnp.float32))
        return attended.astype(jnp.bfloat16).reshape(AGENTS, D)
    attended = lax.map(agent_step, jnp.arange(STEPS))
    residual = residual + jnp.dot(attended.reshape(tokens, D), agent_merge, preferred_element_type=jnp.float32)
    normed = rms_norm(residual).astype(jnp.bfloat16)
    projected = jnp.dot(normed, time_proj, preferred_element_type=jnp.float32).astype(jnp.bfloat16)
    projected = projected.reshape(STEPS, AGENTS, 3 * D)
    time_keys = projected[:, :, D:]
    padded = jnp.concatenate([jnp.zeros((WINDOW, AGENTS, 2 * D), jnp.bfloat16), time_keys], axis=0)
    block_count = STEPS // WINDOW
    previous = padded[:STEPS].reshape(block_count, WINDOW, AGENTS, 2, HEADS, HEAD)
    current = padded[WINDOW:].reshape(block_count, WINDOW, AGENTS, 2, HEADS, HEAD)
    key_blocks = jnp.concatenate([previous, current], axis=1)
    query_blocks = projected[:, :, :D].reshape(block_count, WINDOW, AGENTS, HEADS, HEAD)
    block_starts = jnp.arange(block_count) * WINDOW

    def time_block(inputs):
        query_block, key_block, start_step = inputs
        query_step = start_step + jnp.arange(WINDOW)
        key_step = start_step - WINDOW + jnp.arange(2 * WINDOW)
        allowed = (key_step[None, :] <= query_step[:, None]) & (key_step[None, :] > query_step[:, None] - WINDOW) & (key_step[None, :] >= 0)
        scores = jnp.einsum('qahe,kahe->ahqk', query_block.astype(jnp.float32), key_block[:, :, 0].astype(jnp.float32)) * score_scale
        scores = jnp.where(allowed[None, None], scores, -1e+30)
        attention = softmax_rows(scores).astype(jnp.bfloat16)
        result = jnp.einsum('ahqk,kahe->qahe', attention.astype(jnp.float32), key_block[:, :, 1].astype(jnp.float32))
        return result.astype(jnp.bfloat16)
    attended = lax.map(time_block, (query_blocks, key_blocks, block_starts))
    residual = residual + jnp.dot(attended.reshape(tokens, D), time_merge, preferred_element_type=jnp.float32)
    values = lax.optimization_barrier(jnp.sum(rms_norm(residual) * value_weight, axis=-1)).reshape(STEPS, AGENTS)
    living = 1.0 - done_flags.astype(jnp.float32)
    following = jnp.concatenate([values[1:], bootstrap[None, :]], axis=0)
    changes = rewards + discount * living * following - values
    factors = discount * trace_decay * living

    def backward(running, inputs):
        change, factor = inputs
        running = change + factor * running
        return (running, running)
    final_carry, advantages = lax.scan(backward, jnp.zeros((AGENTS,), jnp.float32), (changes, factors), reverse=True)
    return (values, advantages)
```

```python
import functools
import math

import jax
import jax.numpy as jnp
from jax import lax
from jax.experimental import pallas as pl
from jax.experimental.pallas import tpu as pltpu
from jax.sharding import PartitionSpec as P

HEADS = 8
WINDOW = 16

discount = 0.9997
trace_decay = 0.995
epsilon = 1e-06
NEG = -1e30
MESH = pl.DeviceIdType.MESH


def normed_bf16(x):
    return (x * lax.rsqrt(jnp.mean(x * x, axis=-1, keepdims=True) + epsilon)).astype(jnp.bfloat16)


def dot(a, b):
    return jnp.dot(a, b, preferred_element_type=jnp.float32)


def pair_attention(q, k, v, head, coef, bias=None):
    rows = q.shape[0]
    first = lax.broadcasted_iota(jnp.int32, q.shape, 1) < head
    zero = jnp.zeros_like(q)
    both = jnp.concatenate([jnp.where(first, q, zero), jnp.where(first, zero, q)], axis=0)
    s = lax.dot_general(both, k, (((1,), (1,)), ((), ())), preferred_element_type=jnp.float32)
    s = s * coef
    if bias is not None:
        s = s + bias
    e = jnp.exp2(s - jnp.max(s, axis=-1, keepdims=True))
    o = dot(e.astype(jnp.bfloat16), v) / jnp.sum(e, axis=-1, keepdims=True)
    return jnp.where(first, o[:rows], o[rows:])


def agent_step(x, listed, proj_ref, merge_ref, tproj_ref, head):
    width = x.shape[-1]
    coef = head**-0.5 * math.log2(math.e)
    x = x.astype(jnp.float32)
    own = dot(normed_bf16(x), proj_ref[...]).astype(jnp.bfloat16)
    other = dot(normed_bf16(listed.astype(jnp.float32)), proj_ref[:, width:]).astype(jnp.bfloat16)
    outs = []
    for lo in range(0, width, 2 * head):
        hi = lo + 2 * head
        k = jnp.concatenate([own[:, width + lo : width + hi], other[:, lo:hi]], axis=0)
        v = jnp.concatenate(
            [own[:, 2 * width + lo : 2 * width + hi], other[:, width + lo : width + hi]], axis=0
        )
        outs.append(pair_attention(own[:, lo:hi], k, v, head, coef))
    mix = jnp.concatenate(outs, axis=1).astype(jnp.bfloat16)
    res = x + dot(mix, merge_ref[...])
    return res, dot(normed_bf16(res), tproj_ref[...]).astype(jnp.bfloat16)


def agent_kernel(head, listing, pos, x_ref, *refs):
    listed = [r[0] for r in refs[:listing]]
    proj, merge, tproj, res_ref, qkv_ref = refs[listing:]
    res, qkv = agent_step(x_ref[0], jnp.concatenate(listed, axis=0), proj, merge, tproj, head)
    res_ref[0] = res
    qkv_ref[0] = qkv


def agent_call(embedded, arrived, positions, proj, merge, tproj, head):
    steps, agents, width = embedded.shape
    listing = positions.shape[0] // steps
    block = (1, agents, width)
    whole = lambda a: pl.BlockSpec(a.shape, lambda t, p: (0, 0))
    pick = lambda j: pl.BlockSpec(block, lambda t, p: (p[t * listing + j], 0, 0))
    return pl.pallas_call(
        functools.partial(agent_kernel, head, listing),
        grid_spec=pltpu.PrefetchScalarGridSpec(
            num_scalar_prefetch=1,
            grid=(steps,),
            in_specs=[pl.BlockSpec(block, lambda t, p: (t, 0, 0))]
            + [pick(j) for j in range(listing)]
            + [whole(proj), whole(merge), whole(tproj)],
            out_specs=[
                pl.BlockSpec(block, lambda t, p: (t, 0, 0)),
                pl.BlockSpec((1, agents, 3 * width), lambda t, p: (t, 0, 0)),
            ],
        ),
        out_shape=[
            jax.ShapeDtypeStruct((steps, agents, width), jnp.float32),
            jax.ShapeDtypeStruct((steps, agents, 3 * width), jnp.bfloat16),
        ],
        compiler_params=pltpu.CompilerParams(vmem_limit_bytes=40 * 2**20),
        name="agent_attention",
    )(positions, embedded, *([arrived] * listing), proj, merge, tproj)


def time_kernel(head, res_ref, qkv_ref, prev_ref, merge_ref, weight_ref, out_ref, mix_ref):
    steps, agents, width = res_ref.shape
    coef = head**-0.5 * math.log2(math.e)
    oct_ = 8
    rows, cols = steps * oct_, 2 * steps * oct_
    r = lax.broadcasted_iota(jnp.int32, (rows, cols), 0)
    c = lax.broadcasted_iota(jnp.int32, (rows, cols), 1)
    qt, ks = r // oct_, c // oct_ - steps
    seen = (ks <= qt) & (ks > qt - WINDOW) & ((ks >= 0) | (lax.axis_index("tm") > 0))
    bias = jnp.where(seen & (r % oct_ == c % oct_), 0.0, NEG).astype(jnp.float32)
    bias = jnp.concatenate([bias, bias], axis=0)

    def halves(block):
        block = block.astype(jnp.float32)
        return [
            block[:, h : h + oct_].reshape(steps * oct_, block.shape[-1]).astype(jnp.bfloat16)
            for h in (0, oct_)
        ]

    def group(i, _):
        at = pl.ds(pl.multiple_of(i * 2 * oct_, 2 * oct_), 2 * oct_)
        for lo in range(0, width, 2 * head):
            hi = lo + 2 * head
            q = halves(qkv_ref[:, at, lo:hi])
            k0 = halves(prev_ref[:, at, lo:hi])
            k1 = halves(qkv_ref[:, at, width + lo : width + hi])
            v0 = halves(prev_ref[:, at, width + lo : width + hi])
            v1 = halves(qkv_ref[:, at, 2 * width + lo : 2 * width + hi])
            outs = []
            for h in range(2):
                k = jnp.concatenate([k0[h], k1[h]], axis=0)
                v = jnp.concatenate([v0[h], v1[h]], axis=0)
                o = pair_attention(q[h], k, v, head, coef, bias)
                outs.append(o.reshape(steps, oct_, hi - lo))
            mix_ref[:, at, lo:hi] = jnp.concatenate(outs, axis=1).astype(jnp.bfloat16)
        return 0

    lax.fori_loop(0, agents // (2 * oct_), group, 0)

    def finish(t, _):
        res = res_ref[t] + dot(mix_ref[t], merge_ref[...])
        square = res * res
        scaled = res * weight_ref[...]
        lanes = 128
        sq = sum(square[:, j : j + lanes] for j in range(0, width, lanes))
        sc = sum(scaled[:, j : j + lanes] for j in range(0, width, lanes))
        mean = jnp.sum(sq.T, axis=0, keepdims=True) / width
        out_ref[pl.ds(t, 1), :] = jnp.sum(sc.T, axis=0, keepdims=True) * lax.rsqrt(mean + epsilon)
        return 0

    lax.fori_loop(0, steps, finish, 0)


def time_call(res, qkv, prev, merge, weight, head):
    steps, agents, width = res.shape
    return pl.pallas_call(
        functools.partial(time_kernel, head),
        out_shape=jax.ShapeDtypeStruct((steps, agents), jnp.float32),
        in_specs=[pl.BlockSpec(memory_space=pltpu.VMEM)] * 5,
        out_specs=pl.BlockSpec(memory_space=pltpu.VMEM),
        scratch_shapes=[pltpu.VMEM((steps, agents, width), jnp.bfloat16)],
        compiler_params=pltpu.CompilerParams(vmem_limit_bytes=56 * 2**20),
        name="time_attention",
    )(res, qkv, prev, merge, weight.reshape(1, width))


def from_behind(value, axis, by):
    devices = lax.axis_size(axis)
    pairs = [(i, i + by) for i in range(devices) if 0 <= i + by < devices]
    return lax.ppermute(value, axis, pairs)


def advantage_pass(values, done_flags, rewards, bootstrap):
    steps = values.shape[0]
    parts = lax.axis_size("tm")
    last = lax.axis_index("tm") == parts - 1
    living = 1.0 - done_flags.astype(jnp.float32)
    factors = discount * trace_decay * living

    def run(following_last, running):
        following = jnp.concatenate([values[1:], following_last[None]], axis=0)
        changes = rewards + discount * living * following - values
        rows = [None] * steps
        for t in reversed(range(steps)):
            running = changes[t] + factors[t] * running
            rows[t] = running
        return jnp.stack(rows)

    zero = jnp.zeros_like(bootstrap)
    advantages = run(bootstrap, zero)
    for _ in range(parts - 1):
        sent = jnp.stack([values[0], advantages[0]])
        got = from_behind(sent, "tm", -1)
        advantages = run(jnp.where(last, bootstrap, got[0]), jnp.where(last, zero, got[1]))
    return advantages


def take_kernel(index, x_ref, out_ref):
    out_ref[...] = x_ref[...]


def take_steps(embedded, index):
    steps, agents, width = embedded.shape
    block = (1, agents, width)
    return pl.pallas_call(
        take_kernel,
        grid_spec=pltpu.PrefetchScalarGridSpec(
            num_scalar_prefetch=1,
            grid=index.shape,
            in_specs=[pl.BlockSpec(block, lambda i, p: (p[i], 0, 0))],
            out_specs=pl.BlockSpec(block, lambda i, p: (i, 0, 0)),
        ),
        out_shape=jax.ShapeDtypeStruct((index.shape[0], agents, width), embedded.dtype),
        name="take_steps",
    )(index, embedded)


def exchange(embedded, block_lists):
    steps, agents, width = embedded.shape
    listing = block_lists.shape[2]
    blocks = lax.axis_size("agent")
    capacity = max(2, (2 * steps * listing + blocks - 1) // blocks)
    peers = block_lists[0].reshape(-1)
    count = peers.shape[0]
    row_steps = jnp.arange(count, dtype=jnp.int32) // listing
    hits = (peers[:, None] == jnp.arange(blocks, dtype=jnp.int32)[None, :]).astype(jnp.int32)
    order = jnp.arange(count, dtype=jnp.int32)
    before = (order[None, :] < order[:, None]).astype(jnp.int32)
    earlier = jnp.sum(before[:, :, None] * hits[None], axis=1)
    slot = jnp.sum(earlier * hits, axis=1)
    slots = (slot[:, None] == jnp.arange(capacity, dtype=jnp.int32)[None, :]).astype(jnp.int32)
    requests = jnp.sum((hits * row_steps[:, None])[:, :, None] * slots[:, None, :], axis=0)
    wanted = lax.all_to_all(requests, "agent", split_axis=0, concat_axis=0, tiled=True)
    outgoing = take_steps(embedded, wanted.reshape(-1)).reshape(blocks, capacity, agents, width)
    arrived = lax.all_to_all(outgoing, "agent", split_axis=0, concat_axis=0, tiled=True)
    return arrived.reshape(blocks * capacity, agents, width), peers * capacity + slot


PARTS = 4


def partner(me, k, count):
    other, bit = 0, 1
    while bit < count:
        a, b = lax.rem(lax.div(me, bit), 2), lax.rem(lax.div(k, bit), 2)
        other = other + bit * (a + b - 2 * a * b)
        bit *= 2
    return other


def heads_attention(q, k, v, head):
    rows = q.shape[0]
    first = lax.broadcasted_iota(jnp.int32, q.shape, 1) < head
    zero = jnp.zeros_like(q)
    both = jnp.concatenate([jnp.where(first, q, zero), jnp.where(first, zero, q)], axis=0)
    s = lax.dot_general(both, k, (((1,), (1,)), ((), ())), preferred_element_type=jnp.float32)
    e = jnp.exp2(s - jnp.max(s, axis=-1, keepdims=True))
    o = dot(e.astype(jnp.bfloat16), v) * (1.0 / jnp.sum(e, axis=-1, keepdims=True))
    return jnp.where(first, o[:rows], o[rows:])


def step_split_kernel(
    head, x_ref, lists_ref, proj, merge, tproj, tmerge, weight_ref, done_ref, reward_ref, boot_ref,
    values_ref, adv_ref,
    lists_in, lists, arrived, qkv, stage, ret, res_ref, q_ref, kv_ref, prev_ref, mix_ref, sum_ref,
    value_rows, edge_out, edge_in,
    list_send, list_recv, go_send, go_recv, back_send, back_recv, part_send, part_recv,
    kv_send, kv_recv, kvp_send, kvp_recv, list_sem, edge_sem,
):
    steps, agents, width = x_ref.shape
    listing = lists_ref.shape[1]
    blocks = lax.axis_size("agent")
    phases = steps // blocks
    me, tm = lax.axis_index("agent"), lax.axis_index("tm")
    earlier, later = tm > 0, tm < lax.axis_size("tm") - 1
    size = agents // PARTS
    last = phases - 1
    oct_ = 8
    octs = size // oct_
    coef = head**-0.5 * math.log2(math.e)

    barrier = pltpu.get_barrier_semaphore()

    def greet(k, _):
        peer = {"agent": partner(me, k, blocks)}
        pl.semaphore_signal(barrier, inc=1, device_id=peer, device_id_type=MESH)
        return 0

    lax.fori_loop(1, blocks, greet, 0)

    @pl.when(earlier)
    def _():
        pl.semaphore_signal(barrier, inc=1, device_id={"tm": tm - 1}, device_id_type=MESH)

    @pl.when(later)
    def _():
        pl.semaphore_signal(barrier, inc=1, device_id={"tm": tm + 1}, device_id_type=MESH)

    pl.semaphore_wait(barrier, blocks - 1 + earlier.astype(jnp.int32) + later.astype(jnp.int32))

    def remote(src, dst, send, recv, device):
        return pltpu.make_async_remote_copy(
            src_ref=src, dst_ref=dst, send_sem=send, recv_sem=recv,
            device_id=device, device_id_type=MESH,
        )

    def list_copy(k):
        peer = {"agent": partner(me, k, blocks)}
        return remote(lists_ref, lists_in.at[me], list_send.at[k], list_recv.at[k], peer)

    def go_copy(p, k):
        other = partner(me, k, blocks)
        return remote(
            x_ref.at[p * blocks + other], arrived.at[p, me], go_send.at[p, k], go_recv.at[p, k],
            {"agent": other},
        )

    def back_copy(p, k):
        other = partner(me, k, blocks)
        return remote(
            stage.at[p, other], ret.at[p * blocks + me], back_send.at[p, k], back_recv.at[p, k],
            {"agent": other},
        )

    def part_copy(j, k):
        other = partner(me, k, blocks)
        at = pl.ds(pl.multiple_of(j * size, size), size)
        return remote(
            stage.at[last, other, at], ret.at[last * blocks + me, at], part_send.at[j, k],
            part_recv.at[j, k], {"agent": other},
        )

    count = lax.axis_size("tm")
    after, before = {"tm": lax.rem(tm + 1, count)}, {"tm": lax.rem(tm + count - 1, count)}
    pairs = last * blocks // 2

    def kv_copy(i):
        at = pl.ds(pl.multiple_of(i * 2 * oct_, 2 * oct_), 2 * oct_)
        return remote(kv_ref.at[:, at], prev_ref.at[:, at], kv_send.at[i], kv_recv.at[i], after)

    def kv_part_copy(j):
        at, rows = pl.ds(j * octs, octs), pl.ds(last * blocks * oct_, blocks * oct_)
        return remote(
            kv_ref.at[at, rows], prev_ref.at[at, rows], kvp_send.at[j], kvp_recv.at[j], after
        )

    def edge_copy():
        return remote(edge_out, edge_in, edge_sem.at[0], edge_sem.at[1], before)

    def send_lists(k, _):
        list_copy(k).start()
        return 0

    lax.fori_loop(1, blocks, send_lists, 0)

    def send_out(i, _):
        p, k = lax.div(i, blocks), lax.rem(i, blocks)

        @pl.when(k > 0)
        def _():
            go_copy(p, k).start()

        return 0

    lax.fori_loop(0, phases * blocks, send_out, 0)

    for p in range(phases):
        arrived[p, me] = x_ref[p * blocks + me]
    lists_in[me] = lists_ref[...]

    @pl.when(jnp.logical_not(earlier))
    def _():
        def clear(o, _):
            prev_ref[o] = jnp.zeros(prev_ref.shape[1:], prev_ref.dtype)
            return 0

        lax.fori_loop(0, prev_ref.shape[0], clear, 0)

    def got_list(k, _):
        list_copy(k).wait_recv()
        return 0

    lax.fori_loop(1, blocks, got_list, 0)
    to_scalars = pltpu.make_async_copy(lists_in, lists, list_sem)
    to_scalars.start()
    to_scalars.wait()

    def project(p):
        def pair(i, _):
            @pl.when(i > 0)
            def _():
                go_copy(p, 2 * i).wait_recv()

            go_copy(p, 2 * i + 1).wait_recv()
            low = 2 * lax.div(partner(me, 2 * i, blocks), 2)
            x = arrived[p, pl.ds(low, 2)].reshape(2 * agents, width)
            normed = normed_bf16(x.astype(jnp.float32))
            for c in range(3):
                cols = slice(c * width, (c + 1) * width)
                y = dot(normed, proj[:, cols])
                if c == 0:
                    y = y * coef
                qkv[pl.ds(low, 2), :, cols] = y.astype(jnp.bfloat16).reshape(2, agents, width)
            return 0

        lax.fori_loop(0, blocks // 2, pair, 0)

    def attend(p, b):
        chosen = [lists[b, p * blocks + me, j] for j in range(listing)]
        outs = []
        for lo in range(0, width, 2 * head):
            hi = lo + 2 * head

            def keys(offset):
                rows = [qkv[b, :, offset + lo : offset + hi]]
                rows += [qkv[i, :, offset + lo : offset + hi] for i in chosen]
                return jnp.concatenate(rows, axis=0)

            q = qkv[b, :, lo:hi]
            outs.append(heads_attention(q, keys(width), keys(2 * width), head))
        return jnp.concatenate(outs, axis=1).astype(jnp.bfloat16)

    for p in range(phases):
        project(p)

        def answer(i, _, p=p):
            k = blocks - 1 - i
            b = partner(me, k, blocks)
            stage[p, b] = attend(p, b)

            @pl.when(k > 0)
            def _():
                if p < last:
                    back_copy(p, k).start()
                else:
                    part_copy(0, k).start()

            return 0

        lax.fori_loop(0, blocks, answer, 0)
        ret[p * blocks + me] = stage[p, me]

    def send_part(i, _):
        j, k = lax.div(i, blocks), blocks - 1 - lax.rem(i, blocks)

        @pl.when(k > 0)
        def _():
            part_copy(j, k).start()

        return 0

    lax.fori_loop(blocks, PARTS * blocks, send_part, 0)

    def layer(x, mixed, put_res, put_q, put_kv):
        res = x.astype(jnp.float32) + dot(mixed, merge[...])
        put_res(res)
        normed = normed_bf16(res)
        put_q(dot(normed, tproj[:, :width]) * coef)
        put_kv(0, dot(normed, tproj[:, width : 2 * width]))
        put_kv(1, dot(normed, tproj[:, 2 * width :]))

    def by_oct(value, parts, group):
        rows = value.reshape(parts, group, oct_, value.shape[-1])
        return [
            jnp.concatenate([rows[t, o] for t in range(parts)], axis=0) for o in range(group)
        ]

    def early(n, _):
        p, i = lax.div(n, blocks // 2), lax.rem(n, blocks // 2)

        @pl.when(i > 0)
        def _():
            back_copy(p, 2 * i).wait_recv()

        back_copy(p, 2 * i + 1).wait_recv()
        low = p * blocks + 2 * lax.div(partner(me, 2 * i, blocks), 2)
        at = pl.ds(pl.multiple_of(low * oct_, 2 * oct_), 2 * oct_)

        def put(ref, cols):
            def store(value):
                for o, rows in enumerate(by_oct(value, 2, agents // oct_)):
                    ref[o, at, cols] = rows.astype(ref.dtype)

            return store

        def put_kv(c, value):
            put(kv_ref, slice(c * width, (c + 1) * width))(value)

        layer(
            x_ref[pl.ds(low, 2)].reshape(2 * agents, width),
            ret[pl.ds(low, 2)].reshape(2 * agents, width),
            put(res_ref, slice(0, width)), put(q_ref, slice(0, width)), put_kv,
        )

        @pl.when(later)
        def _():
            kv_copy(lax.div(low, 2)).start()

        return 0

    lax.fori_loop(0, pairs, early, 0)

    @pl.when(earlier)
    def _():
        def ready(i, _):
            kv_copy(i).wait_recv()
            return 0

        lax.fori_loop(0, pairs, ready, 0)

    rows = steps * oct_
    qt = lax.broadcasted_iota(jnp.int32, (2 * rows, rows), 0)
    ks = lax.broadcasted_iota(jnp.int32, (2 * rows, rows), 1)
    same = lax.rem(qt, oct_) == lax.rem(ks, oct_)
    own = lax.div(ks, oct_) <= lax.div(lax.rem(qt, rows), oct_)
    bias = jnp.where(same & (own | earlier), 0.0, NEG).astype(jnp.float32)
    lanes = 128

    def time_oct(o, slot):
        q = q_ref[o]
        for lo in range(0, width, 2 * head):
            hi = lo + 2 * head
            first = lax.broadcasted_iota(jnp.int32, (rows, 2 * head), 1) < head
            piece = q[:, lo:hi]
            zero = jnp.zeros_like(piece)
            both = jnp.concatenate(
                [jnp.where(first, piece, zero), jnp.where(first, zero, piece)], axis=0
            )
            k = jnp.concatenate([kv_ref[o, :, lo:hi], prev_ref[o, :, lo:hi]], axis=0)
            v = jnp.concatenate(
                [kv_ref[o, :, width + lo : width + hi], prev_ref[o, :, width + lo : width + hi]],
                axis=0,
            )
            s = lax.dot_general(
                both, k, (((1,), (1,)), ((), ())), preferred_element_type=jnp.float32
            )
            s = jnp.where(own, s[:, :rows], s[:, rows:]) + bias
            e = jnp.exp2(s - jnp.max(s, axis=-1, keepdims=True))
            total = jnp.sum(e, axis=-1, keepdims=True)
            e = jnp.concatenate([jnp.where(own, e, 0.0), jnp.where(own, 0.0, e)], axis=1)
            out = dot(e.astype(jnp.bfloat16), v) * (1.0 / total)
            out = jnp.where(first, out[:rows], out[rows:])
            mix_ref[pl.ds(pl.multiple_of(slot * rows, rows), rows), lo:hi] = out.astype(
                jnp.bfloat16
            )

    def part(j, _):
        def here(k, _):
            part_copy(j, k).wait_recv()
            return 0

        lax.fori_loop(1, blocks, here, 0)
        at = pl.ds(pl.multiple_of(j * size, size), size)
        turn = slice(last * blocks, steps)
        late = slice(last * blocks * oct_, rows)

        def put(ref, cols):
            def store(value):
                for o, piece in enumerate(by_oct(value, blocks, octs)):
                    ref[j * octs + o, late, cols] = piece.astype(ref.dtype)

            return store

        def put_kv(c, value):
            put(kv_ref, slice(c * width, (c + 1) * width))(value)

        layer(
            x_ref[turn, at].reshape(blocks * size, width),
            ret[turn, at].reshape(blocks * size, width),
            put(res_ref, slice(0, width)), put(q_ref, slice(0, width)), put_kv,
        )

        @pl.when(later)
        def _():
            kv_part_copy(j).start()

        @pl.when(earlier)
        def _():
            kv_part_copy(j).wait_recv()

        def each(o, _):
            time_oct(j * octs + o, o)
            return 0

        lax.fori_loop(0, octs, each, 0)
        sum_ref[...] = dot(mix_ref[...], tmerge[...])
        per = lanes // size
        for i in range(steps // per):
            squares, scales = [], []
            for r in range(per):
                for o in range(octs):
                    spot = slice((i * per + r) * oct_, (i * per + r + 1) * oct_)
                    wide = slice(o * rows + spot.start, o * rows + spot.stop)
                    res = res_ref[j * octs + o, spot] + sum_ref[wide]
                    square, scaled = res * res, res * weight_ref[...]
                    squares.append(sum(square[:, lo : lo + lanes] for lo in range(0, width, lanes)))
                    scales.append(sum(scaled[:, lo : lo + lanes] for lo in range(0, width, lanes)))
            square, scaled = jnp.concatenate(squares, axis=0), jnp.concatenate(scales, axis=0)
            mean = jnp.sum(square.T, axis=0, keepdims=True) / width
            value = jnp.sum(scaled.T, axis=0, keepdims=True) * lax.rsqrt(mean + epsilon)
            value_rows[j, i : i + 1] = value
        return 0

    lax.fori_loop(0, PARTS, part, 0)

    per = lanes // size
    where = lax.div(lax.broadcasted_iota(jnp.int32, (steps // per, lanes), 1), size)
    for r in range(per):
        total = jnp.zeros((steps // per, lanes), jnp.float32)
        for j in range(PARTS):
            turned = value_rows[j]
            if (j - r) % per:
                turned = pltpu.roll(turned, ((j - r) % per) * size, 1)
            total = jnp.where(where == j, turned, total)
        for i in range(steps // per):
            values_ref[i * per + r : i * per + r + 1, :] = total[i : i + 1]

    @pl.when(later)
    def _():
        edge_copy().wait_recv()
        edge_out[...] = edge_in[...]

    @pl.when(jnp.logical_not(later))
    def _():
        edge_out[0:1, :] = boot_ref[...]
        edge_out[1:2, :] = jnp.zeros_like(boot_ref)

    value, running = edge_out[0:1, :], edge_out[1:2, :]
    found = []
    for t in reversed(range(steps)):
        living = 1.0 - done_ref[t : t + 1, :].astype(jnp.float32)
        following, value = value, values_ref[t : t + 1, :]
        change = reward_ref[t : t + 1, :] + discount * living * following - value
        running = change + discount * trace_decay * living * running
        found.append(running)
    edge_out[0:1, :] = value
    edge_out[1:2, :] = running

    @pl.when(earlier)
    def _():
        edge_copy().start()

    for t in range(steps):
        adv_ref[t : t + 1, :] = found[steps - 1 - t]

    def drain(k, _):
        list_copy(k).wait_send()
        for p in range(phases):
            go_copy(p, k).wait_send()
            if p < last:
                back_copy(p, k).wait_send()
        for j in range(PARTS):
            part_copy(j, k).wait_send()
        return 0

    lax.fori_loop(1, blocks, drain, 0)

    @pl.when(later)
    def _():
        def gone(i, _):
            kv_copy(i).wait_send()
            return 0

        lax.fori_loop(0, pairs, gone, 0)

        def gone_part(j, _):
            kv_part_copy(j).wait_send()
            return 0

        lax.fori_loop(0, PARTS, gone_part, 0)

    @pl.when(earlier)
    def _():
        edge_copy().wait_send()


def step_split_call(
    embedded, lists, proj, merge, tproj, tmerge, weight, done, rewards, bootstrap, head
):
    steps, agents, width = embedded.shape
    listing = lists.shape[1]
    blocks = lax.axis_size("agent")
    phases = steps // blocks
    size = agents // PARTS
    vmem = pl.BlockSpec(memory_space=pltpu.VMEM)
    dma = pltpu.SemaphoreType.DMA
    out = jax.ShapeDtypeStruct((steps, agents), jnp.float32)
    b16, f32 = jnp.bfloat16, jnp.float32
    pairs = max(1, (phases - 1) * blocks // 2)
    return pl.pallas_call(
        functools.partial(step_split_kernel, head),
        in_specs=[vmem] * 10,
        out_specs=[vmem, vmem],
        out_shape=[out, out],
        scratch_shapes=[
            pltpu.VMEM((blocks, steps, listing), jnp.int32),
            pltpu.SMEM((blocks, steps, listing), jnp.int32),
            pltpu.VMEM((phases, blocks, agents, width), b16),
            pltpu.VMEM((blocks, agents, 3 * width), b16),
            pltpu.VMEM((phases, blocks, agents, width), b16),
            pltpu.VMEM((steps, agents, width), b16),
            pltpu.VMEM((agents // 8, steps * 8, width), f32),
            pltpu.VMEM((agents // 8, steps * 8, width), b16),
            pltpu.VMEM((agents // 8, steps * 8, 2 * width), b16),
            pltpu.VMEM((agents // 8, steps * 8, 2 * width), b16),
            pltpu.VMEM((size * steps, width), b16),
            pltpu.VMEM((size * steps, width), f32),
            pltpu.VMEM((PARTS, steps * size // 128, 128), f32),
            pltpu.VMEM((2, agents), f32),
            pltpu.VMEM((2, agents), f32),
            dma((blocks,)), dma((blocks,)),
            dma((phases, blocks)), dma((phases, blocks)),
            dma((phases, blocks)), dma((phases, blocks)),
            dma((PARTS, blocks)), dma((PARTS, blocks)),
            dma((pairs,)), dma((pairs,)),
            dma((PARTS,)), dma((PARTS,)),
            dma(()), dma((2,)),
        ],
        compiler_params=pltpu.CompilerParams(
            collective_id=0, has_side_effects=True, vmem_limit_bytes=58 * 2**20
        ),
        name="critic_layer",
    )(
        embedded, lists, proj, merge, tproj, tmerge, weight.reshape(1, width),
        done, rewards, bootstrap.reshape(1, agents),
    )


def body(
    embedded,
    block_lists,
    done_flags,
    rewards,
    bootstrap,
    agent_proj,
    agent_merge,
    time_proj,
    time_merge,
    value_weight,
):
    steps, agents, width = embedded.shape
    head = width // HEADS
    assert steps == WINDOW
    blocks = lax.axis_size("agent")
    if steps % blocks == 0 and blocks & (blocks - 1) == 0 and blocks > 1 and agents == 128:
        return tuple(
            step_split_call(
                embedded, block_lists[0], agent_proj, agent_merge, time_proj, time_merge,
                value_weight, done_flags, rewards, bootstrap, head,
            )
        )
    arrived, positions = exchange(embedded, block_lists)
    res, qkv = agent_call(embedded, arrived, positions, agent_proj, agent_merge, time_proj, head)
    prev = from_behind(qkv[:, :, width:], "tm", 1)
    values = time_call(res, qkv, prev, time_merge, value_weight, head)
    return (values, advantage_pass(values, done_flags, rewards, bootstrap))


def solution(mesh):
    placed = (
        P(("groups", "tm"), "agent", None),
        P(("groups", "agent"), "tm", None),
        P(("groups", "tm"), "agent"),
        P(("groups", "tm"), "agent"),
        P(("groups", "agent")),
        P(),
        P(),
        P(),
        P(),
        P(),
    )
    return jax.shard_map(
        body,
        mesh=mesh,
        in_specs=placed,
        out_specs=(P(("groups", "tm"), "agent"), P(("groups", "tm"), "agent")),
        check_vma=False,
    )
```

```python
import functools
import math

import jax
import jax.numpy as jnp
from jax import lax
from jax.experimental import pallas as pl
from jax.experimental.pallas import tpu as pltpu
from jax.sharding import PartitionSpec as P

HEADS = 8
WINDOW = 16

discount = 0.9997
trace_decay = 0.995
epsilon = 1e-06
NEG = -1e30
MESH = pl.DeviceIdType.MESH


def normed_bf16(x):
    return (x * lax.rsqrt(jnp.mean(x * x, axis=-1, keepdims=True) + epsilon)).astype(jnp.bfloat16)


def dot(a, b):
    return jnp.dot(a, b, preferred_element_type=jnp.float32)


def pair_attention(q, k, v, head, coef, bias=None):
    rows = q.shape[0]
    first = lax.broadcasted_iota(jnp.int32, q.shape, 1) < head
    zero = jnp.zeros_like(q)
    both = jnp.concatenate([jnp.where(first, q, zero), jnp.where(first, zero, q)], axis=0)
    s = lax.dot_general(both, k, (((1,), (1,)), ((), ())), preferred_element_type=jnp.float32)
    s = s * coef
    if bias is not None:
        s = s + bias
    e = jnp.exp2(s - jnp.max(s, axis=-1, keepdims=True))
    o = dot(e.astype(jnp.bfloat16), v) / jnp.sum(e, axis=-1, keepdims=True)
    return jnp.where(first, o[:rows], o[rows:])


def agent_step(x, listed, proj_ref, merge_ref, tproj_ref, head):
    width = x.shape[-1]
    coef = head**-0.5 * math.log2(math.e)
    x = x.astype(jnp.float32)
    own = dot(normed_bf16(x), proj_ref[...]).astype(jnp.bfloat16)
    other = dot(normed_bf16(listed.astype(jnp.float32)), proj_ref[:, width:]).astype(jnp.bfloat16)
    outs = []
    for lo in range(0, width, 2 * head):
        hi = lo + 2 * head
        k = jnp.concatenate([own[:, width + lo : width + hi], other[:, lo:hi]], axis=0)
        v = jnp.concatenate(
            [own[:, 2 * width + lo : 2 * width + hi], other[:, width + lo : width + hi]], axis=0
        )
        outs.append(pair_attention(own[:, lo:hi], k, v, head, coef))
    mix = jnp.concatenate(outs, axis=1).astype(jnp.bfloat16)
    res = x + dot(mix, merge_ref[...])
    return res, dot(normed_bf16(res), tproj_ref[...]).astype(jnp.bfloat16)


def agent_kernel(head, listing, pos, x_ref, *refs):
    listed = [r[0] for r in refs[:listing]]
    proj, merge, tproj, res_ref, qkv_ref = refs[listing:]
    res, qkv = agent_step(x_ref[0], jnp.concatenate(listed, axis=0), proj, merge, tproj, head)
    res_ref[0] = res
    qkv_ref[0] = qkv


def agent_call(embedded, arrived, positions, proj, merge, tproj, head):
    steps, agents, width = embedded.shape
    listing = positions.shape[0] // steps
    block = (1, agents, width)
    whole = lambda a: pl.BlockSpec(a.shape, lambda t, p: (0, 0))
    pick = lambda j: pl.BlockSpec(block, lambda t, p: (p[t * listing + j], 0, 0))
    return pl.pallas_call(
        functools.partial(agent_kernel, head, listing),
        grid_spec=pltpu.PrefetchScalarGridSpec(
            num_scalar_prefetch=1,
            grid=(steps,),
            in_specs=[pl.BlockSpec(block, lambda t, p: (t, 0, 0))]
            + [pick(j) for j in range(listing)]
            + [whole(proj), whole(merge), whole(tproj)],
            out_specs=[
                pl.BlockSpec(block, lambda t, p: (t, 0, 0)),
                pl.BlockSpec((1, agents, 3 * width), lambda t, p: (t, 0, 0)),
            ],
        ),
        out_shape=[
            jax.ShapeDtypeStruct((steps, agents, width), jnp.float32),
            jax.ShapeDtypeStruct((steps, agents, 3 * width), jnp.bfloat16),
        ],
        compiler_params=pltpu.CompilerParams(vmem_limit_bytes=40 * 2**20),
        name="agent_attention",
    )(positions, embedded, *([arrived] * listing), proj, merge, tproj)


def time_kernel(head, res_ref, qkv_ref, prev_ref, merge_ref, weight_ref, out_ref, mix_ref):
    steps, agents, width = res_ref.shape
    coef = head**-0.5 * math.log2(math.e)
    oct_ = 8
    rows, cols = steps * oct_, 2 * steps * oct_
    r = lax.broadcasted_iota(jnp.int32, (rows, cols), 0)
    c = lax.broadcasted_iota(jnp.int32, (rows, cols), 1)
    qt, ks = r // oct_, c // oct_ - steps
    seen = (ks <= qt) & (ks > qt - WINDOW) & ((ks >= 0) | (lax.axis_index("tm") > 0))
    bias = jnp.where(seen & (r % oct_ == c % oct_), 0.0, NEG).astype(jnp.float32)
    bias = jnp.concatenate([bias, bias], axis=0)

    def halves(block):
        block = block.astype(jnp.float32)
        return [
            block[:, h : h + oct_].reshape(steps * oct_, block.shape[-1]).astype(jnp.bfloat16)
            for h in (0, oct_)
        ]

    def group(i, _):
        at = pl.ds(pl.multiple_of(i * 2 * oct_, 2 * oct_), 2 * oct_)
        for lo in range(0, width, 2 * head):
            hi = lo + 2 * head
            q = halves(qkv_ref[:, at, lo:hi])
            k0 = halves(prev_ref[:, at, lo:hi])
            k1 = halves(qkv_ref[:, at, width + lo : width + hi])
            v0 = halves(prev_ref[:, at, width + lo : width + hi])
            v1 = halves(qkv_ref[:, at, 2 * width + lo : 2 * width + hi])
            outs = []
            for h in range(2):
                k = jnp.concatenate([k0[h], k1[h]], axis=0)
                v = jnp.concatenate([v0[h], v1[h]], axis=0)
                o = pair_attention(q[h], k, v, head, coef, bias)
                outs.append(o.reshape(steps, oct_, hi - lo))
            mix_ref[:, at, lo:hi] = jnp.concatenate(outs, axis=1).astype(jnp.bfloat16)
        return 0

    lax.fori_loop(0, agents // (2 * oct_), group, 0)

    def finish(t, _):
        res = res_ref[t] + dot(mix_ref[t], merge_ref[...])
        square = res * res
        scaled = res * weight_ref[...]
        lanes = 128
        sq = sum(square[:, j : j + lanes] for j in range(0, width, lanes))
        sc = sum(scaled[:, j : j + lanes] for j in range(0, width, lanes))
        mean = jnp.sum(sq.T, axis=0, keepdims=True) / width
        out_ref[pl.ds(t, 1), :] = jnp.sum(sc.T, axis=0, keepdims=True) * lax.rsqrt(mean + epsilon)
        return 0

    lax.fori_loop(0, steps, finish, 0)


def time_call(res, qkv, prev, merge, weight, head):
    steps, agents, width = res.shape
    return pl.pallas_call(
        functools.partial(time_kernel, head),
        out_shape=jax.ShapeDtypeStruct((steps, agents), jnp.float32),
        in_specs=[pl.BlockSpec(memory_space=pltpu.VMEM)] * 5,
        out_specs=pl.BlockSpec(memory_space=pltpu.VMEM),
        scratch_shapes=[pltpu.VMEM((steps, agents, width), jnp.bfloat16)],
        compiler_params=pltpu.CompilerParams(vmem_limit_bytes=56 * 2**20),
        name="time_attention",
    )(res, qkv, prev, merge, weight.reshape(1, width))


def from_behind(value, axis, by):
    devices = lax.axis_size(axis)
    pairs = [(i, i + by) for i in range(devices) if 0 <= i + by < devices]
    return lax.ppermute(value, axis, pairs)


def advantage_pass(values, done_flags, rewards, bootstrap):
    steps = values.shape[0]
    parts = lax.axis_size("tm")
    last = lax.axis_index("tm") == parts - 1
    living = 1.0 - done_flags.astype(jnp.float32)
    factors = discount * trace_decay * living

    def run(following_last, running):
        following = jnp.concatenate([values[1:], following_last[None]], axis=0)
        changes = rewards + discount * living * following - values
        rows = [None] * steps
        for t in reversed(range(steps)):
            running = changes[t] + factors[t] * running
            rows[t] = running
        return jnp.stack(rows)

    zero = jnp.zeros_like(bootstrap)
    advantages = run(bootstrap, zero)
    for _ in range(parts - 1):
        sent = jnp.stack([values[0], advantages[0]])
        got = from_behind(sent, "tm", -1)
        advantages = run(jnp.where(last, bootstrap, got[0]), jnp.where(last, zero, got[1]))
    return advantages


def take_kernel(index, x_ref, out_ref):
    out_ref[...] = x_ref[...]


def take_steps(embedded, index):
    steps, agents, width = embedded.shape
    block = (1, agents, width)
    return pl.pallas_call(
        take_kernel,
        grid_spec=pltpu.PrefetchScalarGridSpec(
            num_scalar_prefetch=1,
            grid=index.shape,
            in_specs=[pl.BlockSpec(block, lambda i, p: (p[i], 0, 0))],
            out_specs=pl.BlockSpec(block, lambda i, p: (i, 0, 0)),
        ),
        out_shape=jax.ShapeDtypeStruct((index.shape[0], agents, width), embedded.dtype),
        name="take_steps",
    )(index, embedded)


def exchange(embedded, block_lists):
    steps, agents, width = embedded.shape
    listing = block_lists.shape[2]
    blocks = lax.axis_size("agent")
    capacity = max(2, (2 * steps * listing + blocks - 1) // blocks)
    peers = block_lists[0].reshape(-1)
    count = peers.shape[0]
    row_steps = jnp.arange(count, dtype=jnp.int32) // listing
    hits = (peers[:, None] == jnp.arange(blocks, dtype=jnp.int32)[None, :]).astype(jnp.int32)
    order = jnp.arange(count, dtype=jnp.int32)
    before = (order[None, :] < order[:, None]).astype(jnp.int32)
    earlier = jnp.sum(before[:, :, None] * hits[None], axis=1)
    slot = jnp.sum(earlier * hits, axis=1)
    slots = (slot[:, None] == jnp.arange(capacity, dtype=jnp.int32)[None, :]).astype(jnp.int32)
    requests = jnp.sum((hits * row_steps[:, None])[:, :, None] * slots[:, None, :], axis=0)
    wanted = lax.all_to_all(requests, "agent", split_axis=0, concat_axis=0, tiled=True)
    outgoing = take_steps(embedded, wanted.reshape(-1)).reshape(blocks, capacity, agents, width)
    arrived = lax.all_to_all(outgoing, "agent", split_axis=0, concat_axis=0, tiled=True)
    return arrived.reshape(blocks * capacity, agents, width), peers * capacity + slot


OCT = 8
SHARES = (4, 4, 4, 4)


def parts_of(agents):
    unit, parts, start = agents // sum(SHARES), [], 0
    for share in SHARES:
        parts.append((start, share * unit))
        start += share * unit
    return parts


def partner(me, k, count):
    other, bit = 0, 1
    while bit < count:
        a, b = lax.rem(lax.div(me, bit), 2), lax.rem(lax.div(k, bit), 2)
        other = other + bit * (a + b - 2 * a * b)
        bit *= 2
    return other


def weighted(e, v, first):
    rows, wide = first.shape
    both = dot(e, jnp.concatenate([v, jnp.ones_like(v)], axis=1))
    o = both[:, :wide] / both[:, wide:]
    return jnp.where(first, o[:rows], o[rows:])


def heads_attention(q, k, v, head):
    rows = q.shape[0]
    first = lax.broadcasted_iota(jnp.int32, q.shape, 1) < head
    zero = jnp.zeros_like(q)
    both = jnp.concatenate([jnp.where(first, q, zero), jnp.where(first, zero, q)], axis=0)
    s = lax.dot_general(both, k, (((1,), (1,)), ((), ())), preferred_element_type=jnp.float32)
    e = jnp.exp2(s - jnp.max(s, axis=-1, keepdims=True))
    return weighted(e.astype(jnp.bfloat16), v, first)


def step_split_kernel(
    head, x_in, lists_ref, proj_in, merge_in, tproj_in, tmerge_in, weight_in, done_in, reward_in,
    boot_in, out_ref,
    x_ref, proj, merge, tproj, tmerge, weight_ref, done_ref, reward_ref, boot_ref,
    lists_in, lists, arrived, qkv, stage, ret, res_ref, q_ref, kv_ref, prev_ref, mix_ref, sum_ref,
    own_ref, edge_out, edge_in,
    list_send, list_recv, go_send, go_recv, back_send, back_recv, part_send, part_recv,
    kv_send, kv_recv, kvp_send, kvp_recv, list_sem, edge_sem, load_sem,
):
    values_ref, adv_ref = out_ref.at[0], out_ref.at[1]
    steps, agents, width = x_in.shape
    listing = lists_ref.shape[0]
    blocks = lax.axis_size("agent")
    phases = steps // blocks
    me, tm = lax.axis_index("agent"), lax.axis_index("tm")
    earlier, later = tm > 0, tm < lax.axis_size("tm") - 1
    parts = parts_of(agents)
    last, final = phases - 1, len(parts) - 1
    oct_ = OCT
    coef = head**-0.5 * math.log2(math.e)

    barrier = pltpu.get_barrier_semaphore()

    def greet(k, _):
        peer = {"agent": partner(me, k, blocks)}
        pl.semaphore_signal(barrier, inc=1, device_id=peer, device_id_type=MESH)
        return 0

    lax.fori_loop(1, blocks, greet, 0)

    @pl.when(earlier)
    def _():
        pl.semaphore_signal(barrier, inc=1, device_id={"tm": tm - 1}, device_id_type=MESH)

    @pl.when(later)
    def _():
        pl.semaphore_signal(barrier, inc=1, device_id={"tm": tm + 1}, device_id_type=MESH)

    pl.semaphore_wait(barrier, blocks - 1 + earlier.astype(jnp.int32) + later.astype(jnp.int32))

    def remote(src, dst, send, recv, device):
        return pltpu.make_async_remote_copy(
            src_ref=src, dst_ref=dst, send_sem=send, recv_sem=recv,
            device_id=device, device_id_type=MESH,
        )

    def list_copy(k):
        peer = {"agent": partner(me, k, blocks)}
        return remote(lists_ref, lists_in.at[me], list_send.at[k], list_recv.at[k], peer)

    def go_copy(p, k):
        other = partner(me, k, blocks)
        return remote(
            x_in.at[p * blocks + other], arrived.at[p, me], go_send.at[p, k], go_recv.at[p, k],
            {"agent": other},
        )

    def back_copy(p, k):
        other = partner(me, k, blocks)
        return remote(
            stage.at[p, other], ret.at[p * blocks + me], back_send.at[p, k], back_recv.at[p, k],
            {"agent": other},
        )

    def part_copy(j, k):
        other = partner(me, k, blocks)
        at = pl.ds(*parts[j])
        return remote(
            stage.at[last, other, at], ret.at[last * blocks + me, at], part_send.at[j, k],
            part_recv.at[j, k], {"agent": other},
        )

    count = lax.axis_size("tm")
    after, before = {"tm": lax.rem(tm + 1, count)}, {"tm": lax.rem(tm + count - 1, count)}
    pairs = last * blocks // 2

    def kv_copy(i):
        at = pl.ds(pl.multiple_of(i * 2 * oct_, 2 * oct_), 2 * oct_)
        return remote(kv_ref.at[:, at], prev_ref.at[:, at], kv_send.at[i], kv_recv.at[i], after)

    def kv_part_copy(j):
        start, size = parts[j]
        at, rows = pl.ds(start // oct_, size // oct_), pl.ds(last * blocks * oct_, blocks * oct_)
        return remote(
            kv_ref.at[at, rows], prev_ref.at[at, rows], kvp_send.at[j], kvp_recv.at[j], after
        )

    def edge_copy():
        return remote(edge_out, edge_in, edge_sem.at[0], edge_sem.at[1], before)

    def send_lists(k, _):
        list_copy(k).start()
        return 0

    lax.fori_loop(1, blocks, send_lists, 0)

    def send_out(i, _):
        p, k = lax.div(i, blocks), lax.rem(i, blocks)

        @pl.when(k > 0)
        def _():
            go_copy(p, k).start()

        return 0

    lax.fori_loop(0, phases * blocks, send_out, 0)

    mine = [
        pltpu.make_async_copy(x_in.at[p * blocks + me], arrived.at[p, me], load_sem.at[p])
        for p in range(phases)
    ]
    outside = [proj_in, merge_in, tproj_in, tmerge_in, x_in, weight_in, done_in, reward_in, boot_in]
    inside = [proj, merge, tproj, tmerge, x_ref, weight_ref, done_ref, reward_ref, boot_ref]
    loads = [
        pltpu.make_async_copy(a, b, load_sem.at[phases + i])
        for i, (a, b) in enumerate(zip(outside, inside))
    ]
    for load in mine + loads:
        load.start()
    lists_in[me] = lists_ref[...]

    @pl.when(jnp.logical_not(earlier))
    def _():
        def clear(o, _):
            prev_ref[o] = jnp.zeros(prev_ref.shape[1:], prev_ref.dtype)
            return 0

        lax.fori_loop(0, prev_ref.shape[0], clear, 0)

    def got_list(k, _):
        list_copy(k).wait_recv()
        return 0

    lax.fori_loop(1, blocks, got_list, 0)
    to_scalars = pltpu.make_async_copy(lists_in, lists, list_sem)
    to_scalars.start()
    to_scalars.wait()

    for load in mine + loads[:1]:
        load.wait()

    def project(p):
        def pair(i, _):
            @pl.when(i > 0)
            def _():
                go_copy(p, 2 * i).wait_recv()

            go_copy(p, 2 * i + 1).wait_recv()
            low = 2 * lax.div(partner(me, 2 * i, blocks), 2)
            x = arrived[p, pl.ds(low, 2)].reshape(2 * agents, width)
            normed = normed_bf16(x.astype(jnp.float32))
            for c in range(3):
                cols = slice(c * width, (c + 1) * width)
                y = dot(normed, proj[:, cols])
                if c == 0:
                    y = y * coef
                qkv[pl.ds(low, 2), :, cols] = y.astype(jnp.bfloat16).reshape(2, agents, width)
            return 0

        lax.fori_loop(0, blocks // 2, pair, 0)

    def attend(p, b):
        chosen = [lists[b, j, p * blocks + me] for j in range(listing)]
        outs = []
        for lo in range(0, width, 2 * head):
            hi = lo + 2 * head

            def keys(offset):
                rows = [qkv[b, :, offset + lo : offset + hi]]
                rows += [qkv[i, :, offset + lo : offset + hi] for i in chosen]
                return jnp.concatenate(rows, axis=0)

            q = qkv[b, :, lo:hi]
            outs.append(heads_attention(q, keys(width), keys(2 * width), head))
        return jnp.concatenate(outs, axis=1).astype(jnp.bfloat16)

    for p in range(phases):
        project(p)

        def answer(i, _, p=p):
            k = blocks - 1 - i
            b = partner(me, k, blocks)
            stage[p, b] = attend(p, b)

            @pl.when(k > 0)
            def _():
                if p < last:
                    back_copy(p, k).start()
                else:
                    part_copy(0, k).start()

            return 0

        lax.fori_loop(0, blocks, answer, 0)
        ret[p * blocks + me] = stage[p, me]

    for j in range(1, final + 1):

        def send_part(i, _, j=j):
            part_copy(j, blocks - 1 - i).start()
            return 0

        lax.fori_loop(0, blocks - 1, send_part, 0)

    for load in loads[1:]:
        load.wait()

    def layer(x, mixed, put_res, put_q, put_kv, send):
        res = x.astype(jnp.float32) + dot(mixed, merge[...])
        put_res(res)
        normed = normed_bf16(res)
        put_kv(0, dot(normed, tproj[:, width : 2 * width]))
        put_kv(1, dot(normed, tproj[:, 2 * width :]))
        pl.when(later)(send)
        put_q(dot(normed, tproj[:, :width]) * coef)

    def by_oct(value, parts, group):
        rows = value.reshape(parts, group, oct_, value.shape[-1])
        return [
            jnp.concatenate([rows[t, o] for t in range(parts)], axis=0) for o in range(group)
        ]

    def early(n, _):
        p, i = lax.div(n, blocks // 2), lax.rem(n, blocks // 2)

        @pl.when(i > 0)
        def _():
            back_copy(p, 2 * i).wait_recv()

        back_copy(p, 2 * i + 1).wait_recv()
        low = p * blocks + 2 * lax.div(partner(me, 2 * i, blocks), 2)
        at = pl.ds(pl.multiple_of(low * oct_, 2 * oct_), 2 * oct_)

        def put(ref, cols):
            def store(value):
                for o, rows in enumerate(by_oct(value, 2, agents // oct_)):
                    ref[o, at, cols] = rows.astype(ref.dtype)

            return store

        def put_kv(c, value):
            put(kv_ref, slice(c * width, (c + 1) * width))(value)

        layer(
            x_ref[pl.ds(low, 2)].reshape(2 * agents, width),
            ret[pl.ds(low, 2)].reshape(2 * agents, width),
            put(res_ref, slice(0, width)), put(q_ref, slice(0, width)), put_kv,
            lambda: kv_copy(lax.div(low, 2)).start(),
        )

        return 0

    lax.fori_loop(0, pairs, early, 0)

    @pl.when(earlier)
    def _():
        def ready(i, _):
            kv_copy(i).wait_recv()
            return 0

        lax.fori_loop(0, pairs, ready, 0)

    rows = steps * oct_
    qt = lax.broadcasted_iota(jnp.int32, (2 * rows, rows), 0)
    ks = lax.broadcasted_iota(jnp.int32, (2 * rows, rows), 1)
    same = lax.rem(qt, oct_) == lax.rem(ks, oct_)
    own = lax.div(ks, oct_) <= lax.div(lax.rem(qt, rows), oct_)
    bias = jnp.where(same & (own | earlier), 0.0, NEG).astype(jnp.float32)
    own_ref[...] = jnp.where(own, 1.0, 0.0).astype(jnp.float32).astype(jnp.bfloat16)
    lanes = 128
    first = lax.broadcasted_iota(jnp.int32, (rows, 2 * head), 1) < head

    def time_oct(o, slot):
        q = q_ref[o]
        for lo in range(0, width, 2 * head):
            hi = lo + 2 * head
            piece = q[:, lo:hi]
            zero = jnp.zeros_like(piece)
            both = jnp.concatenate(
                [jnp.where(first, piece, zero), jnp.where(first, zero, piece)], axis=0
            )
            k = jnp.concatenate([kv_ref[o, :, lo:hi], prev_ref[o, :, lo:hi]], axis=0)
            v = jnp.concatenate(
                [kv_ref[o, :, width + lo : width + hi], prev_ref[o, :, width + lo : width + hi]],
                axis=0,
            )
            s = lax.dot_general(
                both, k, (((1,), (1,)), ((), ())), preferred_element_type=jnp.float32
            )
            s = jnp.where(own, s[:, :rows], s[:, rows:]) + bias
            e = jnp.exp2(s - jnp.max(s, axis=-1, keepdims=True)).astype(jnp.bfloat16)
            here = e * own_ref[...]
            out = weighted(jnp.concatenate([here, e - here], axis=1), v, first)
            mix_ref[slot * rows : (slot + 1) * rows, lo:hi] = out.astype(jnp.bfloat16)

    def front(j):
        start, size = parts[j]
        octs = size // oct_

        def here(k, _):
            part_copy(j, k).wait_recv()
            return 0

        lax.fori_loop(1, blocks, here, 0)
        at = pl.ds(start, size)
        turn = slice(last * blocks, steps)
        late = slice(last * blocks * oct_, rows)

        def put(ref, cols):
            def store(value):
                for o, piece in enumerate(by_oct(value, blocks, octs)):
                    ref[start // oct_ + o, late, cols] = piece.astype(ref.dtype)

            return store

        def put_kv(c, value):
            put(kv_ref, slice(c * width, (c + 1) * width))(value)

        layer(
            x_ref[turn, at].reshape(blocks * size, width),
            ret[turn, at].reshape(blocks * size, width),
            put(res_ref, slice(0, width)), put(q_ref, slice(0, width)), put_kv,
            lambda: kv_part_copy(j).start(),
        )

    lane = lax.broadcasted_iota(jnp.int32, (1, lanes), 1)

    def back(j):
        start, size = parts[j]
        octs = size // oct_

        @pl.when(earlier)
        def _():
            kv_part_copy(j).wait_recv()

        for o in range(octs):
            time_oct(start // oct_ + o, o)
        used = slice(0, octs * rows)
        sum_ref[used] = dot(mix_ref[used], tmerge[...])
        per = lanes // size
        inside = (lane >= start) & (lane < start + size)
        for i in range(steps // per):
            squares, scales = [], []
            for r in range(per):
                for o in range(octs):
                    spot = slice((i * per + r) * oct_, (i * per + r + 1) * oct_)
                    wide = slice(o * rows + spot.start, o * rows + spot.stop)
                    res = res_ref[start // oct_ + o, spot] + sum_ref[wide]
                    square, scaled = res * res, res * weight_ref[...]
                    squares.append(sum(square[:, lo : lo + lanes] for lo in range(0, width, lanes)))
                    scales.append(sum(scaled[:, lo : lo + lanes] for lo in range(0, width, lanes)))
            square, scaled = jnp.concatenate(squares, axis=0), jnp.concatenate(scales, axis=0)
            mean = jnp.sum(square.T, axis=0, keepdims=True) / width
            value = jnp.sum(scaled.T, axis=0, keepdims=True) * lax.rsqrt(mean + epsilon)
            value = jnp.broadcast_to(value, (oct_, lanes))
            for r in range(per):
                shift = (start - r * size) % lanes
                turned = pltpu.roll(value, shift, 1) if shift else value
                t = i * per + r
                if j > 0:
                    kept = values_ref[t : t + 1, :]
                    values_ref[t : t + 1, :] = jnp.where(inside, turned[:1], kept)
                else:
                    values_ref[t : t + 1, :] = turned[:1]

    for j in range(final + 1):
        if j == final:
            back(j - 1)
        front(j)
        if 0 < j < final:
            back(j - 1)
    back(final)

    running, gain = jnp.zeros((1, agents), jnp.float32), jnp.ones((1, agents), jnp.float32)
    found, gains = [], []
    following = jnp.zeros((1, agents), jnp.float32)
    for t in reversed(range(steps)):
        living = 1.0 - done_ref[t : t + 1, :].astype(jnp.float32)
        value = values_ref[t : t + 1, :]
        change = reward_ref[t : t + 1, :] + discount * living * following - value
        running = change + discount * trace_decay * living * running
        gain = gain * (discount * living if t == steps - 1 else discount * trace_decay * living)
        following = value
        found.append(running)
        gains.append(gain)

    @pl.when(later)
    def _():
        edge_copy().wait_recv()
        edge_out[...] = edge_in[...]

    @pl.when(jnp.logical_not(later))
    def _():
        edge_out[0:1, :] = boot_ref[...]
        edge_out[1:2, :] = jnp.zeros_like(boot_ref)

    beyond = edge_out[0:1, :] + trace_decay * edge_out[1:2, :]
    edge_out[0:1, :] = value
    edge_out[1:2, :] = running + gain * beyond

    @pl.when(earlier)
    def _():
        edge_copy().start()

    for t in range(steps):
        adv_ref[t : t + 1, :] = found[steps - 1 - t] + gains[steps - 1 - t] * beyond

    def drain(k, _):
        list_copy(k).wait_send()
        for p in range(phases):
            go_copy(p, k).wait_send()
            if p < last:
                back_copy(p, k).wait_send()
        for j in range(final + 1):
            part_copy(j, k).wait_send()
        return 0

    lax.fori_loop(1, blocks, drain, 0)

    @pl.when(later)
    def _():
        def gone(i, _):
            kv_copy(i).wait_send()
            return 0

        lax.fori_loop(0, pairs, gone, 0)

        for j in range(final + 1):
            kv_part_copy(j).wait_send()

    @pl.when(earlier)
    def _():
        edge_copy().wait_send()


def step_split_call(
    embedded, lists, proj, merge, tproj, tmerge, weight, done, rewards, bootstrap, head
):
    steps, agents, width = embedded.shape
    listing = lists.shape[0]
    blocks = lax.axis_size("agent")
    phases = steps // blocks
    parts = len(SHARES)
    size = max(part[1] for part in parts_of(agents))
    vmem, hbm = pl.BlockSpec(memory_space=pltpu.VMEM), pl.BlockSpec(memory_space=pl.ANY)
    dma = pltpu.SemaphoreType.DMA
    out = jax.ShapeDtypeStruct((2, steps, agents), jnp.float32)
    b16, f32 = jnp.bfloat16, jnp.float32
    pairs = max(1, (phases - 1) * blocks // 2)
    return pl.pallas_call(
        functools.partial(step_split_kernel, head),
        in_specs=[hbm, vmem] + [hbm] * 8,
        out_specs=vmem,
        out_shape=out,
        scratch_shapes=[
            pltpu.VMEM((steps, agents, width), b16),
            pltpu.VMEM((width, 3 * width), b16),
            pltpu.VMEM((width, width), b16),
            pltpu.VMEM((width, 3 * width), b16),
            pltpu.VMEM((width, width), b16),
            pltpu.VMEM((1, width), f32),
            pltpu.VMEM((steps, agents), jnp.int32),
            pltpu.VMEM((steps, agents), f32),
            pltpu.VMEM((1, agents), f32),
            pltpu.VMEM((blocks, listing, steps), jnp.int32),
            pltpu.SMEM((blocks, listing, steps), jnp.int32),
            pltpu.VMEM((phases, blocks, agents, width), b16),
            pltpu.VMEM((blocks, agents, 3 * width), b16),
            pltpu.VMEM((phases, blocks, agents, width), b16),
            pltpu.VMEM((steps, agents, width), b16),
            pltpu.VMEM((agents // 8, steps * 8, width), f32),
            pltpu.VMEM((agents // 8, steps * 8, width), b16),
            pltpu.VMEM((agents // 8, steps * 8, 2 * width), b16),
            pltpu.VMEM((agents // 8, steps * 8, 2 * width), b16),
            pltpu.VMEM((size * steps, width), b16),
            pltpu.VMEM((size * steps, width), f32),
            pltpu.VMEM((2 * 8 * steps, 8 * steps), b16),
            pltpu.VMEM((2, agents), f32),
            pltpu.VMEM((2, agents), f32),
            dma((blocks,)), dma((blocks,)),
            dma((phases, blocks)), dma((phases, blocks)),
            dma((phases, blocks)), dma((phases, blocks)),
            dma((parts, blocks)), dma((parts, blocks)),
            dma((pairs,)), dma((pairs,)),
            dma((parts,)), dma((parts,)),
            dma(()), dma((2,)), dma((phases + 9,)),
        ],
        compiler_params=pltpu.CompilerParams(
            collective_id=0, has_side_effects=True, vmem_limit_bytes=58 * 2**20
        ),
        name="critic_layer",
    )(
        embedded, lists, proj, merge, tproj, tmerge, weight.reshape(1, width),
        done, rewards, bootstrap.reshape(1, agents),
    )


def body(
    embedded,
    block_lists,
    done_flags,
    rewards,
    bootstrap,
    agent_proj,
    agent_merge,
    time_proj,
    time_merge,
    value_weight,
):
    steps, agents, width = embedded.shape
    head = width // HEADS
    assert steps == WINDOW
    blocks = lax.axis_size("agent")
    if steps % blocks == 0 and blocks & (blocks - 1) == 0 and blocks > 1 and agents == 128:
        both = (
            step_split_call(
                embedded, block_lists[0].T, agent_proj, agent_merge, time_proj, time_merge,
                value_weight, done_flags, rewards, bootstrap, head,
            )
        )
        return both[0], both[1]
    arrived, positions = exchange(embedded, block_lists)
    res, qkv = agent_call(embedded, arrived, positions, agent_proj, agent_merge, time_proj, head)
    prev = from_behind(qkv[:, :, width:], "tm", 1)
    values = time_call(res, qkv, prev, time_merge, value_weight, head)
    return (values, advantage_pass(values, done_flags, rewards, bootstrap))


def solution(mesh):
    placed = (
        P(("groups", "tm"), "agent", None),
        P(("groups", "agent"), "tm", None),
        P(("groups", "tm"), "agent"),
        P(("groups", "tm"), "agent"),
        P(("groups", "agent")),
        P(),
        P(),
        P(),
        P(),
        P(),
    )
    return jax.shard_map(
        body,
        mesh=mesh,
        in_specs=placed,
        out_specs=(P(("groups", "tm"), "agent"), P(("groups", "tm"), "agent")),
        check_vma=False,
    )
```

```python
import functools
import math

import jax
import jax.numpy as jnp
from jax import lax
from jax.experimental import pallas as pl
from jax.experimental.pallas import tpu as pltpu
from jax.sharding import PartitionSpec as P

HEADS = 8
WINDOW = 16

discount = 0.9997
trace_decay = 0.995
epsilon = 1e-06
NEG = -1e30
MESH = pl.DeviceIdType.MESH


def normed_bf16(x):
    return (x * lax.rsqrt(jnp.mean(x * x, axis=-1, keepdims=True) + epsilon)).astype(jnp.bfloat16)


def dot(a, b):
    return jnp.dot(a, b, preferred_element_type=jnp.float32)


def pair_attention(q, k, v, head, coef, bias=None):
    rows = q.shape[0]
    first = lax.broadcasted_iota(jnp.int32, q.shape, 1) < head
    zero = jnp.zeros_like(q)
    both = jnp.concatenate([jnp.where(first, q, zero), jnp.where(first, zero, q)], axis=0)
    s = lax.dot_general(both, k, (((1,), (1,)), ((), ())), preferred_element_type=jnp.float32)
    s = s * coef
    if bias is not None:
        s = s + bias
    e = jnp.exp2(s - jnp.max(s, axis=-1, keepdims=True))
    o = dot(e.astype(jnp.bfloat16), v) / jnp.sum(e, axis=-1, keepdims=True)
    return jnp.where(first, o[:rows], o[rows:])


def agent_step(x, listed, proj_ref, merge_ref, tproj_ref, head):
    width = x.shape[-1]
    coef = head**-0.5 * math.log2(math.e)
    x = x.astype(jnp.float32)
    own = dot(normed_bf16(x), proj_ref[...]).astype(jnp.bfloat16)
    other = dot(normed_bf16(listed.astype(jnp.float32)), proj_ref[:, width:]).astype(jnp.bfloat16)
    outs = []
    for lo in range(0, width, 2 * head):
        hi = lo + 2 * head
        k = jnp.concatenate([own[:, width + lo : width + hi], other[:, lo:hi]], axis=0)
        v = jnp.concatenate(
            [own[:, 2 * width + lo : 2 * width + hi], other[:, width + lo : width + hi]], axis=0
        )
        outs.append(pair_attention(own[:, lo:hi], k, v, head, coef))
    mix = jnp.concatenate(outs, axis=1).astype(jnp.bfloat16)
    res = x + dot(mix, merge_ref[...])
    return res, dot(normed_bf16(res), tproj_ref[...]).astype(jnp.bfloat16)


def agent_kernel(head, listing, pos, x_ref, *refs):
    listed = [r[0] for r in refs[:listing]]
    proj, merge, tproj, res_ref, qkv_ref = refs[listing:]
    res, qkv = agent_step(x_ref[0], jnp.concatenate(listed, axis=0), proj, merge, tproj, head)
    res_ref[0] = res
    qkv_ref[0] = qkv


def agent_call(embedded, arrived, positions, proj, merge, tproj, head):
    steps, agents, width = embedded.shape
    listing = positions.shape[0] // steps
    block = (1, agents, width)
    whole = lambda a: pl.BlockSpec(a.shape, lambda t, p: (0, 0))
    pick = lambda j: pl.BlockSpec(block, lambda t, p: (p[t * listing + j], 0, 0))
    return pl.pallas_call(
        functools.partial(agent_kernel, head, listing),
        grid_spec=pltpu.PrefetchScalarGridSpec(
            num_scalar_prefetch=1,
            grid=(steps,),
            in_specs=[pl.BlockSpec(block, lambda t, p: (t, 0, 0))]
            + [pick(j) for j in range(listing)]
            + [whole(proj), whole(merge), whole(tproj)],
            out_specs=[
                pl.BlockSpec(block, lambda t, p: (t, 0, 0)),
                pl.BlockSpec((1, agents, 3 * width), lambda t, p: (t, 0, 0)),
            ],
        ),
        out_shape=[
            jax.ShapeDtypeStruct((steps, agents, width), jnp.float32),
            jax.ShapeDtypeStruct((steps, agents, 3 * width), jnp.bfloat16),
        ],
        compiler_params=pltpu.CompilerParams(vmem_limit_bytes=40 * 2**20),
        name="agent_attention",
    )(positions, embedded, *([arrived] * listing), proj, merge, tproj)


def time_kernel(head, res_ref, qkv_ref, prev_ref, merge_ref, weight_ref, out_ref, mix_ref):
    steps, agents, width = res_ref.shape
    coef = head**-0.5 * math.log2(math.e)
    oct_ = 8
    rows, cols = steps * oct_, 2 * steps * oct_
    r = lax.broadcasted_iota(jnp.int32, (rows, cols), 0)
    c = lax.broadcasted_iota(jnp.int32, (rows, cols), 1)
    qt, ks = r // oct_, c // oct_ - steps
    seen = (ks <= qt) & (ks > qt - WINDOW) & ((ks >= 0) | (lax.axis_index("tm") > 0))
    bias = jnp.where(seen & (r % oct_ == c % oct_), 0.0, NEG).astype(jnp.float32)
    bias = jnp.concatenate([bias, bias], axis=0)

    def halves(block):
        block = block.astype(jnp.float32)
        return [
            block[:, h : h + oct_].reshape(steps * oct_, block.shape[-1]).astype(jnp.bfloat16)
            for h in (0, oct_)
        ]

    def group(i, _):
        at = pl.ds(pl.multiple_of(i * 2 * oct_, 2 * oct_), 2 * oct_)
        for lo in range(0, width, 2 * head):
            hi = lo + 2 * head
            q = halves(qkv_ref[:, at, lo:hi])
            k0 = halves(prev_ref[:, at, lo:hi])
            k1 = halves(qkv_ref[:, at, width + lo : width + hi])
            v0 = halves(prev_ref[:, at, width + lo : width + hi])
            v1 = halves(qkv_ref[:, at, 2 * width + lo : 2 * width + hi])
            outs = []
            for h in range(2):
                k = jnp.concatenate([k0[h], k1[h]], axis=0)
                v = jnp.concatenate([v0[h], v1[h]], axis=0)
                o = pair_attention(q[h], k, v, head, coef, bias)
                outs.append(o.reshape(steps, oct_, hi - lo))
            mix_ref[:, at, lo:hi] = jnp.concatenate(outs, axis=1).astype(jnp.bfloat16)
        return 0

    lax.fori_loop(0, agents // (2 * oct_), group, 0)

    def finish(t, _):
        res = res_ref[t] + dot(mix_ref[t], merge_ref[...])
        square = res * res
        scaled = res * weight_ref[...]
        lanes = 128
        sq = sum(square[:, j : j + lanes] for j in range(0, width, lanes))
        sc = sum(scaled[:, j : j + lanes] for j in range(0, width, lanes))
        mean = jnp.sum(sq.T, axis=0, keepdims=True) / width
        out_ref[pl.ds(t, 1), :] = jnp.sum(sc.T, axis=0, keepdims=True) * lax.rsqrt(mean + epsilon)
        return 0

    lax.fori_loop(0, steps, finish, 0)


def time_call(res, qkv, prev, merge, weight, head):
    steps, agents, width = res.shape
    return pl.pallas_call(
        functools.partial(time_kernel, head),
        out_shape=jax.ShapeDtypeStruct((steps, agents), jnp.float32),
        in_specs=[pl.BlockSpec(memory_space=pltpu.VMEM)] * 5,
        out_specs=pl.BlockSpec(memory_space=pltpu.VMEM),
        scratch_shapes=[pltpu.VMEM((steps, agents, width), jnp.bfloat16)],
        compiler_params=pltpu.CompilerParams(vmem_limit_bytes=56 * 2**20),
        name="time_attention",
    )(res, qkv, prev, merge, weight.reshape(1, width))


def from_behind(value, axis, by):
    devices = lax.axis_size(axis)
    pairs = [(i, i + by) for i in range(devices) if 0 <= i + by < devices]
    return lax.ppermute(value, axis, pairs)


def advantage_pass(values, done_flags, rewards, bootstrap):
    steps = values.shape[0]
    parts = lax.axis_size("tm")
    last = lax.axis_index("tm") == parts - 1
    living = 1.0 - done_flags.astype(jnp.float32)
    factors = discount * trace_decay * living

    def run(following_last, running):
        following = jnp.concatenate([values[1:], following_last[None]], axis=0)
        changes = rewards + discount * living * following - values
        rows = [None] * steps
        for t in reversed(range(steps)):
            running = changes[t] + factors[t] * running
            rows[t] = running
        return jnp.stack(rows)

    zero = jnp.zeros_like(bootstrap)
    advantages = run(bootstrap, zero)
    for _ in range(parts - 1):
        sent = jnp.stack([values[0], advantages[0]])
        got = from_behind(sent, "tm", -1)
        advantages = run(jnp.where(last, bootstrap, got[0]), jnp.where(last, zero, got[1]))
    return advantages


def take_kernel(index, x_ref, out_ref):
    out_ref[...] = x_ref[...]


def take_steps(embedded, index):
    steps, agents, width = embedded.shape
    block = (1, agents, width)
    return pl.pallas_call(
        take_kernel,
        grid_spec=pltpu.PrefetchScalarGridSpec(
            num_scalar_prefetch=1,
            grid=index.shape,
            in_specs=[pl.BlockSpec(block, lambda i, p: (p[i], 0, 0))],
            out_specs=pl.BlockSpec(block, lambda i, p: (i, 0, 0)),
        ),
        out_shape=jax.ShapeDtypeStruct((index.shape[0], agents, width), embedded.dtype),
        name="take_steps",
    )(index, embedded)


def exchange(embedded, block_lists):
    steps, agents, width = embedded.shape
    listing = block_lists.shape[2]
    blocks = lax.axis_size("agent")
    capacity = max(2, (2 * steps * listing + blocks - 1) // blocks)
    peers = block_lists[0].reshape(-1)
    count = peers.shape[0]
    row_steps = jnp.arange(count, dtype=jnp.int32) // listing
    hits = (peers[:, None] == jnp.arange(blocks, dtype=jnp.int32)[None, :]).astype(jnp.int32)
    order = jnp.arange(count, dtype=jnp.int32)
    before = (order[None, :] < order[:, None]).astype(jnp.int32)
    earlier = jnp.sum(before[:, :, None] * hits[None], axis=1)
    slot = jnp.sum(earlier * hits, axis=1)
    slots = (slot[:, None] == jnp.arange(capacity, dtype=jnp.int32)[None, :]).astype(jnp.int32)
    requests = jnp.sum((hits * row_steps[:, None])[:, :, None] * slots[:, None, :], axis=0)
    wanted = lax.all_to_all(requests, "agent", split_axis=0, concat_axis=0, tiled=True)
    outgoing = take_steps(embedded, wanted.reshape(-1)).reshape(blocks, capacity, agents, width)
    arrived = lax.all_to_all(outgoing, "agent", split_axis=0, concat_axis=0, tiled=True)
    return arrived.reshape(blocks * capacity, agents, width), peers * capacity + slot


OCT = 8
SHARES = (4, 4, 4, 2, 2)


def parts_of(agents):
    unit, parts, start = agents // sum(SHARES), [], 0
    for share in SHARES:
        parts.append((start, share * unit))
        start += share * unit
    return parts


def partner(me, k, count):
    other, bit = 0, 1
    while bit < count:
        a, b = lax.rem(lax.div(me, bit), 2), lax.rem(lax.div(k, bit), 2)
        other = other + bit * (a + b - 2 * a * b)
        bit *= 2
    return other


def weighted(e, v, first):
    rows, wide = first.shape
    both = dot(e, jnp.concatenate([v, jnp.ones_like(v)], axis=1))
    o = both[:, :wide] / both[:, wide:]
    return jnp.where(first, o[:rows], o[rows:])


def heads_attention(q, k, v, head):
    rows = q.shape[0]
    first = lax.broadcasted_iota(jnp.int32, q.shape, 1) < head
    zero = jnp.zeros_like(q)
    both = jnp.concatenate([jnp.where(first, q, zero), jnp.where(first, zero, q)], axis=0)
    s = lax.dot_general(both, k, (((1,), (1,)), ((), ())), preferred_element_type=jnp.float32)
    e = jnp.exp2(s - jnp.max(s, axis=-1, keepdims=True))
    return weighted(e.astype(jnp.bfloat16), v, first)


def step_split_kernel(
    head, x_in, lists_ref, proj_in, merge_in, tproj_in, tmerge_in, weight_in, done_in, reward_in,
    boot_in, out_ref,
    x_ref, proj, merge, tproj, tmerge, weight_ref, done_ref, reward_ref, boot_ref,
    lists_in, lists, arrived, qkv, stage, ret, res_ref, q_ref, kv_ref, prev_ref, mix_ref, sum_ref,
    own_ref, edge_out, edge_in,
    list_send, list_recv, go_send, go_recv, back_send, back_recv, part_send, part_recv,
    kv_send, kv_recv, kvp_send, kvp_recv, list_sem, edge_sem, load_sem,
):
    values_ref, adv_ref = out_ref.at[0], out_ref.at[1]
    steps, agents, width = x_in.shape
    listing = lists_ref.shape[0]
    blocks = lax.axis_size("agent")
    phases = steps // blocks
    me, tm = lax.axis_index("agent"), lax.axis_index("tm")
    earlier, later = tm > 0, tm < lax.axis_size("tm") - 1
    parts = parts_of(agents)
    last, final = phases - 1, len(parts) - 1
    oct_ = OCT
    coef = head**-0.5 * math.log2(math.e)

    barrier = pltpu.get_barrier_semaphore()

    def greet(k, _):
        peer = {"agent": partner(me, k, blocks)}
        pl.semaphore_signal(barrier, inc=1, device_id=peer, device_id_type=MESH)
        return 0

    lax.fori_loop(1, blocks, greet, 0)

    @pl.when(earlier)
    def _():
        pl.semaphore_signal(barrier, inc=1, device_id={"tm": tm - 1}, device_id_type=MESH)

    @pl.when(later)
    def _():
        pl.semaphore_signal(barrier, inc=1, device_id={"tm": tm + 1}, device_id_type=MESH)

    pl.semaphore_wait(barrier, blocks - 1 + earlier.astype(jnp.int32) + later.astype(jnp.int32))

    def remote(src, dst, send, recv, device):
        return pltpu.make_async_remote_copy(
            src_ref=src, dst_ref=dst, send_sem=send, recv_sem=recv,
            device_id=device, device_id_type=MESH,
        )

    def list_copy(k):
        peer = {"agent": partner(me, k, blocks)}
        return remote(lists_ref, lists_in.at[me], list_send.at[k], list_recv.at[k], peer)

    def go_copy(p, k):
        other = partner(me, k, blocks)
        return remote(
            x_in.at[p * blocks + other], arrived.at[p, me], go_send.at[p, k], go_recv.at[p, k],
            {"agent": other},
        )

    def back_copy(p, k):
        other = partner(me, k, blocks)
        return remote(
            stage.at[p, other], ret.at[p * blocks + me], back_send.at[p, k], back_recv.at[p, k],
            {"agent": other},
        )

    def part_copy(j, k):
        other = partner(me, k, blocks)
        at = pl.ds(*parts[j])
        return remote(
            stage.at[last, other, at], ret.at[last * blocks + me, at], part_send.at[j, k],
            part_recv.at[j, k], {"agent": other},
        )

    count = lax.axis_size("tm")
    after, before = {"tm": lax.rem(tm + 1, count)}, {"tm": lax.rem(tm + count - 1, count)}
    pairs = last * blocks // 2

    def kv_copy(i):
        at = pl.ds(pl.multiple_of(i * 2 * oct_, 2 * oct_), 2 * oct_)
        return remote(kv_ref.at[:, at], prev_ref.at[:, at], kv_send.at[i], kv_recv.at[i], after)

    def kv_part_copy(j):
        start, size = parts[j]
        at, rows = pl.ds(start // oct_, size // oct_), pl.ds(last * blocks * oct_, blocks * oct_)
        return remote(
            kv_ref.at[at, rows], prev_ref.at[at, rows], kvp_send.at[j], kvp_recv.at[j], after
        )

    def edge_copy():
        return remote(edge_out, edge_in, edge_sem.at[0], edge_sem.at[1], before)

    def send_lists(k, _):
        list_copy(k).start()
        return 0

    lax.fori_loop(1, blocks, send_lists, 0)

    def send_out(i, _):
        p, k = lax.div(i, blocks), lax.rem(i, blocks)

        @pl.when(k > 0)
        def _():
            go_copy(p, k).start()

        return 0

    lax.fori_loop(0, phases * blocks, send_out, 0)

    mine = [
        pltpu.make_async_copy(x_in.at[p * blocks + me], arrived.at[p, me], load_sem.at[p])
        for p in range(phases)
    ]
    outside = [proj_in, merge_in, tproj_in, tmerge_in, x_in, weight_in, done_in, reward_in, boot_in]
    inside = [proj, merge, tproj, tmerge, x_ref, weight_ref, done_ref, reward_ref, boot_ref]
    loads = [
        pltpu.make_async_copy(a, b, load_sem.at[phases + i])
        for i, (a, b) in enumerate(zip(outside, inside))
    ]
    for load in mine + loads:
        load.start()
    lists_in[me] = lists_ref[...]

    @pl.when(jnp.logical_not(earlier))
    def _():
        def clear(o, _):
            prev_ref[o] = jnp.zeros(prev_ref.shape[1:], prev_ref.dtype)
            return 0

        lax.fori_loop(0, prev_ref.shape[0], clear, 0)

    def got_list(k, _):
        list_copy(k).wait_recv()
        return 0

    lax.fori_loop(1, blocks, got_list, 0)
    to_scalars = pltpu.make_async_copy(lists_in, lists, list_sem)
    to_scalars.start()
    to_scalars.wait()

    for load in mine + loads[:1]:
        load.wait()

    def project(p):
        def pair(i, _):
            @pl.when(i > 0)
            def _():
                go_copy(p, 2 * i).wait_recv()

            go_copy(p, 2 * i + 1).wait_recv()
            low = 2 * lax.div(partner(me, 2 * i, blocks), 2)
            x = arrived[p, pl.ds(low, 2)].reshape(2 * agents, width)
            normed = normed_bf16(x.astype(jnp.float32))
            for c in range(3):
                cols = slice(c * width, (c + 1) * width)
                y = dot(normed, proj[:, cols])
                if c == 0:
                    y = y * coef
                qkv[pl.ds(low, 2), :, cols] = y.astype(jnp.bfloat16).reshape(2, agents, width)
            return 0

        lax.fori_loop(0, blocks // 2, pair, 0)

    def attend(p, b):
        chosen = [lists[b, j, p * blocks + me] for j in range(listing)]
        outs = []
        for lo in range(0, width, 2 * head):
            hi = lo + 2 * head

            def keys(offset):
                rows = [qkv[b, :, offset + lo : offset + hi]]
                rows += [qkv[i, :, offset + lo : offset + hi] for i in chosen]
                return jnp.concatenate(rows, axis=0)

            q = qkv[b, :, lo:hi]
            outs.append(heads_attention(q, keys(width), keys(2 * width), head))
        return jnp.concatenate(outs, axis=1).astype(jnp.bfloat16)

    for p in range(phases):
        project(p)

        def answer(i, _, p=p):
            k = blocks - 1 - i
            b = partner(me, k, blocks)
            stage[p, b] = attend(p, b)

            @pl.when(k > 0)
            def _():
                if p < last:
                    back_copy(p, k).start()
                else:
                    part_copy(0, k).start()

            return 0

        lax.fori_loop(0, blocks, answer, 0)
        ret[p * blocks + me] = stage[p, me]

    ahead = 2

    def send_part(j):
        def one(i, _):
            part_copy(j, blocks - 1 - i).start()
            return 0

        lax.fori_loop(0, blocks - 1, one, 0)

    for j in range(1, min(ahead, final + 1)):
        send_part(j)

    for load in loads[1:]:
        load.wait()

    def layer(x, mixed, put_res, put_q, put_kv, send):
        res = x.astype(jnp.float32) + dot(mixed, merge[...])
        put_res(res)
        normed = normed_bf16(res)
        put_kv(0, dot(normed, tproj[:, width : 2 * width]))
        put_kv(1, dot(normed, tproj[:, 2 * width :]))
        pl.when(later)(send)
        put_q(dot(normed, tproj[:, :width]) * coef)

    def by_oct(value, parts, group):
        rows = value.reshape(parts, group, oct_, value.shape[-1])
        return [
            jnp.concatenate([rows[t, o] for t in range(parts)], axis=0) for o in range(group)
        ]

    def early(n, _):
        p, i = lax.div(n, blocks // 2), lax.rem(n, blocks // 2)

        @pl.when(i > 0)
        def _():
            back_copy(p, 2 * i).wait_recv()

        back_copy(p, 2 * i + 1).wait_recv()
        low = p * blocks + 2 * lax.div(partner(me, 2 * i, blocks), 2)
        at = pl.ds(pl.multiple_of(low * oct_, 2 * oct_), 2 * oct_)

        def put(ref, cols):
            def store(value):
                for o, rows in enumerate(by_oct(value, 2, agents // oct_)):
                    ref[o, at, cols] = rows.astype(ref.dtype)

            return store

        def put_kv(c, value):
            put(kv_ref, slice(c * width, (c + 1) * width))(value)

        layer(
            x_ref[pl.ds(low, 2)].reshape(2 * agents, width),
            ret[pl.ds(low, 2)].reshape(2 * agents, width),
            put(res_ref, slice(0, width)), put(q_ref, slice(0, width)), put_kv,
            lambda: kv_copy(lax.div(low, 2)).start(),
        )

        return 0

    lax.fori_loop(0, pairs, early, 0)

    @pl.when(earlier)
    def _():
        def ready(i, _):
            kv_copy(i).wait_recv()
            return 0

        lax.fori_loop(0, pairs, ready, 0)

    rows = steps * oct_
    qt = lax.broadcasted_iota(jnp.int32, (2 * rows, rows), 0)
    ks = lax.broadcasted_iota(jnp.int32, (2 * rows, rows), 1)
    same = lax.rem(qt, oct_) == lax.rem(ks, oct_)
    own = lax.div(ks, oct_) <= lax.div(lax.rem(qt, rows), oct_)
    bias = jnp.where(same & (own | earlier), 0.0, NEG).astype(jnp.float32)
    own_ref[...] = jnp.where(own, 1.0, 0.0).astype(jnp.float32).astype(jnp.bfloat16)
    lanes = 128
    first = lax.broadcasted_iota(jnp.int32, (rows, 2 * head), 1) < head

    def time_oct(o, slot):
        q = q_ref[o]
        for lo in range(0, width, 2 * head):
            hi = lo + 2 * head
            piece = q[:, lo:hi]
            zero = jnp.zeros_like(piece)
            both = jnp.concatenate(
                [jnp.where(first, piece, zero), jnp.where(first, zero, piece)], axis=0
            )
            k = jnp.concatenate([kv_ref[o, :, lo:hi], prev_ref[o, :, lo:hi]], axis=0)
            v = jnp.concatenate(
                [kv_ref[o, :, width + lo : width + hi], prev_ref[o, :, width + lo : width + hi]],
                axis=0,
            )
            s = lax.dot_general(
                both, k, (((1,), (1,)), ((), ())), preferred_element_type=jnp.float32
            )
            s = jnp.where(own, s[:, :rows], s[:, rows:]) + bias
            e = jnp.exp2(s - jnp.max(s, axis=-1, keepdims=True)).astype(jnp.bfloat16)
            here = e * own_ref[...]
            out = weighted(jnp.concatenate([here, e - here], axis=1), v, first)
            mix_ref[slot * rows : (slot + 1) * rows, lo:hi] = out.astype(jnp.bfloat16)

    def front(j):
        start, size = parts[j]
        octs = size // oct_

        def here(k, _):
            part_copy(j, k).wait_recv()
            return 0

        lax.fori_loop(1, blocks, here, 0)
        at = pl.ds(start, size)
        turn = slice(last * blocks, steps)
        late = slice(last * blocks * oct_, rows)

        def put(ref, cols):
            def store(value):
                for o, piece in enumerate(by_oct(value, blocks, octs)):
                    ref[start // oct_ + o, late, cols] = piece.astype(ref.dtype)

            return store

        def put_kv(c, value):
            put(kv_ref, slice(c * width, (c + 1) * width))(value)

        layer(
            x_ref[turn, at].reshape(blocks * size, width),
            ret[turn, at].reshape(blocks * size, width),
            put(res_ref, slice(0, width)), put(q_ref, slice(0, width)), put_kv,
            lambda: kv_part_copy(j).start(),
        )

    lane = lax.broadcasted_iota(jnp.int32, (1, lanes), 1)

    def back(j):
        start, size = parts[j]
        octs = size // oct_

        @pl.when(earlier)
        def _():
            kv_part_copy(j).wait_recv()

        for o in range(octs):
            time_oct(start // oct_ + o, o)
        used = slice(0, octs * rows)
        sum_ref[used] = dot(mix_ref[used], tmerge[...])
        per = lanes // size
        inside = (lane >= start) & (lane < start + size)
        for i in range(steps // per):
            squares, scales = [], []
            for r in range(per):
                for o in range(octs):
                    spot = slice((i * per + r) * oct_, (i * per + r + 1) * oct_)
                    wide = slice(o * rows + spot.start, o * rows + spot.stop)
                    res = res_ref[start // oct_ + o, spot] + sum_ref[wide]
                    square, scaled = res * res, res * weight_ref[...]
                    squares.append(sum(square[:, lo : lo + lanes] for lo in range(0, width, lanes)))
                    scales.append(sum(scaled[:, lo : lo + lanes] for lo in range(0, width, lanes)))
            square, scaled = jnp.concatenate(squares, axis=0), jnp.concatenate(scales, axis=0)
            mean = jnp.sum(square.T, axis=0, keepdims=True) / width
            value = jnp.sum(scaled.T, axis=0, keepdims=True) * lax.rsqrt(mean + epsilon)
            value = jnp.broadcast_to(value, (oct_, lanes))
            for r in range(per):
                shift = (start - r * size) % lanes
                turned = pltpu.roll(value, shift, 1) if shift else value
                t = i * per + r
                if j > 0:
                    kept = values_ref[t : t + 1, :]
                    values_ref[t : t + 1, :] = jnp.where(inside, turned[:1], kept)
                else:
                    values_ref[t : t + 1, :] = turned[:1]

    for j in range(final + 1):
        if j == final:
            back(j - 1)
        front(j)
        if j + ahead <= final:

            def gone(k, _, j=j):
                part_copy(j, k).wait_send()
                return 0

            lax.fori_loop(1, blocks, gone, 0)
            send_part(j + ahead)
        if 0 < j < final:
            back(j - 1)
    back(final)

    running, gain = jnp.zeros((1, agents), jnp.float32), jnp.ones((1, agents), jnp.float32)
    found, gains = [], []
    following = jnp.zeros((1, agents), jnp.float32)
    for t in reversed(range(steps)):
        living = 1.0 - done_ref[t : t + 1, :].astype(jnp.float32)
        value = values_ref[t : t + 1, :]
        change = reward_ref[t : t + 1, :] + discount * living * following - value
        running = change + discount * trace_decay * living * running
        gain = gain * (discount * living if t == steps - 1 else discount * trace_decay * living)
        following = value
        found.append(running)
        gains.append(gain)

    @pl.when(later)
    def _():
        edge_copy().wait_recv()
        edge_out[...] = edge_in[...]

    @pl.when(jnp.logical_not(later))
    def _():
        edge_out[0:1, :] = boot_ref[...]
        edge_out[1:2, :] = jnp.zeros_like(boot_ref)

    beyond = edge_out[0:1, :] + trace_decay * edge_out[1:2, :]
    edge_out[0:1, :] = value
    edge_out[1:2, :] = running + gain * beyond

    @pl.when(earlier)
    def _():
        edge_copy().start()

    for t in range(steps):
        adv_ref[t : t + 1, :] = found[steps - 1 - t] + gains[steps - 1 - t] * beyond

    def drain(k, _):
        list_copy(k).wait_send()
        for p in range(phases):
            go_copy(p, k).wait_send()
            if p < last:
                back_copy(p, k).wait_send()
        for j in range(max(0, final + 1 - ahead), final + 1):
            part_copy(j, k).wait_send()
        return 0

    lax.fori_loop(1, blocks, drain, 0)

    @pl.when(later)
    def _():
        def gone(i, _):
            kv_copy(i).wait_send()
            return 0

        lax.fori_loop(0, pairs, gone, 0)

        for j in range(final + 1):
            kv_part_copy(j).wait_send()

    @pl.when(earlier)
    def _():
        edge_copy().wait_send()


def step_split_call(
    embedded, lists, proj, merge, tproj, tmerge, weight, done, rewards, bootstrap, head
):
    steps, agents, width = embedded.shape
    listing = lists.shape[0]
    blocks = lax.axis_size("agent")
    phases = steps // blocks
    parts = len(SHARES)
    size = max(part[1] for part in parts_of(agents))
    vmem, hbm = pl.BlockSpec(memory_space=pltpu.VMEM), pl.BlockSpec(memory_space=pl.ANY)
    dma = pltpu.SemaphoreType.DMA
    out = jax.ShapeDtypeStruct((2, steps, agents), jnp.float32)
    b16, f32 = jnp.bfloat16, jnp.float32
    pairs = max(1, (phases - 1) * blocks // 2)
    return pl.pallas_call(
        functools.partial(step_split_kernel, head),
        in_specs=[hbm, vmem] + [hbm] * 8,
        out_specs=vmem,
        out_shape=out,
        scratch_shapes=[
            pltpu.VMEM((steps, agents, width), b16),
            pltpu.VMEM((width, 3 * width), b16),
            pltpu.VMEM((width, width), b16),
            pltpu.VMEM((width, 3 * width), b16),
            pltpu.VMEM((width, width), b16),
            pltpu.VMEM((1, width), f32),
            pltpu.VMEM((steps, agents), jnp.int32),
            pltpu.VMEM((steps, agents), f32),
            pltpu.VMEM((1, agents), f32),
            pltpu.VMEM((blocks, listing, steps), jnp.int32),
            pltpu.SMEM((blocks, listing, steps), jnp.int32),
            pltpu.VMEM((phases, blocks, agents, width), b16),
            pltpu.VMEM((blocks, agents, 3 * width), b16),
            pltpu.VMEM((phases, blocks, agents, width), b16),
            pltpu.VMEM((steps, agents, width), b16),
            pltpu.VMEM((agents // 8, steps * 8, width), f32),
            pltpu.VMEM((agents // 8, steps * 8, width), b16),
            pltpu.VMEM((agents // 8, steps * 8, 2 * width), b16),
            pltpu.VMEM((agents // 8, steps * 8, 2 * width), b16),
            pltpu.VMEM((size * steps, width), b16),
            pltpu.VMEM((size * steps, width), f32),
            pltpu.VMEM((2 * 8 * steps, 8 * steps), b16),
            pltpu.VMEM((2, agents), f32),
            pltpu.VMEM((2, agents), f32),
            dma((blocks,)), dma((blocks,)),
            dma((phases, blocks)), dma((phases, blocks)),
            dma((phases, blocks)), dma((phases, blocks)),
            dma((parts, blocks)), dma((parts, blocks)),
            dma((pairs,)), dma((pairs,)),
            dma((parts,)), dma((parts,)),
            dma(()), dma((2,)), dma((phases + 9,)),
        ],
        compiler_params=pltpu.CompilerParams(
            collective_id=0, has_side_effects=True, vmem_limit_bytes=58 * 2**20
        ),
        name="critic_layer",
    )(
        embedded, lists, proj, merge, tproj, tmerge, weight.reshape(1, width),
        done, rewards, bootstrap.reshape(1, agents),
    )


def body(
    embedded,
    block_lists,
    done_flags,
    rewards,
    bootstrap,
    agent_proj,
    agent_merge,
    time_proj,
    time_merge,
    value_weight,
):
    steps, agents, width = embedded.shape
    head = width // HEADS
    assert steps == WINDOW
    blocks = lax.axis_size("agent")
    if steps % blocks == 0 and blocks & (blocks - 1) == 0 and blocks > 1 and agents == 128:
        both = (
            step_split_call(
                embedded, block_lists[0].T, agent_proj, agent_merge, time_proj, time_merge,
                value_weight, done_flags, rewards, bootstrap, head,
            )
        )
        return both[0], both[1]
    arrived, positions = exchange(embedded, block_lists)
    res, qkv = agent_call(embedded, arrived, positions, agent_proj, agent_merge, time_proj, head)
    prev = from_behind(qkv[:, :, width:], "tm", 1)
    values = time_call(res, qkv, prev, time_merge, value_weight, head)
    return (values, advantage_pass(values, done_flags, rewards, bootstrap))


def solution(mesh):
    placed = (
        P(("groups", "tm"), "agent", None),
        P(("groups", "agent"), "tm", None),
        P(("groups", "tm"), "agent"),
        P(("groups", "tm"), "agent"),
        P(("groups", "agent")),
        P(),
        P(),
        P(),
        P(),
        P(),
    )
    return jax.shard_map(
        body,
        mesh=mesh,
        in_specs=placed,
        out_specs=(P(("groups", "tm"), "agent"), P(("groups", "tm"), "agent")),
        check_vma=False,
    )
```

```python
import functools
import math

import jax
import jax.numpy as jnp
from jax import lax
from jax.experimental import pallas as pl
from jax.experimental.pallas import tpu as pltpu
from jax.sharding import PartitionSpec as P

HEADS = 8
WINDOW = 16

discount = 0.9997
trace_decay = 0.995
epsilon = 1e-06
NEG = -1e30
MESH = pl.DeviceIdType.MESH


def normed_bf16(x):
    return (x * lax.rsqrt(jnp.mean(x * x, axis=-1, keepdims=True) + epsilon)).astype(jnp.bfloat16)


def dot(a, b):
    return jnp.dot(a, b, preferred_element_type=jnp.float32)


def pair_attention(q, k, v, head, coef, bias=None):
    rows = q.shape[0]
    first = lax.broadcasted_iota(jnp.int32, q.shape, 1) < head
    zero = jnp.zeros_like(q)
    both = jnp.concatenate([jnp.where(first, q, zero), jnp.where(first, zero, q)], axis=0)
    s = lax.dot_general(both, k, (((1,), (1,)), ((), ())), preferred_element_type=jnp.float32)
    s = s * coef
    if bias is not None:
        s = s + bias
    e = jnp.exp2(s - jnp.max(s, axis=-1, keepdims=True))
    o = dot(e.astype(jnp.bfloat16), v) / jnp.sum(e, axis=-1, keepdims=True)
    return jnp.where(first, o[:rows], o[rows:])


def agent_step(x, listed, proj_ref, merge_ref, tproj_ref, head):
    width = x.shape[-1]
    coef = head**-0.5 * math.log2(math.e)
    x = x.astype(jnp.float32)
    own = dot(normed_bf16(x), proj_ref[...]).astype(jnp.bfloat16)
    other = dot(normed_bf16(listed.astype(jnp.float32)), proj_ref[:, width:]).astype(jnp.bfloat16)
    outs = []
    for lo in range(0, width, 2 * head):
        hi = lo + 2 * head
        k = jnp.concatenate([own[:, width + lo : width + hi], other[:, lo:hi]], axis=0)
        v = jnp.concatenate(
            [own[:, 2 * width + lo : 2 * width + hi], other[:, width + lo : width + hi]], axis=0
        )
        outs.append(pair_attention(own[:, lo:hi], k, v, head, coef))
    mix = jnp.concatenate(outs, axis=1).astype(jnp.bfloat16)
    res = x + dot(mix, merge_ref[...])
    return res, dot(normed_bf16(res), tproj_ref[...]).astype(jnp.bfloat16)


def agent_kernel(head, listing, pos, x_ref, *refs):
    listed = [r[0] for r in refs[:listing]]
    proj, merge, tproj, res_ref, qkv_ref = refs[listing:]
    res, qkv = agent_step(x_ref[0], jnp.concatenate(listed, axis=0), proj, merge, tproj, head)
    res_ref[0] = res
    qkv_ref[0] = qkv


def agent_call(embedded, arrived, positions, proj, merge, tproj, head):
    steps, agents, width = embedded.shape
    listing = positions.shape[0] // steps
    block = (1, agents, width)
    whole = lambda a: pl.BlockSpec(a.shape, lambda t, p: (0, 0))
    pick = lambda j: pl.BlockSpec(block, lambda t, p: (p[t * listing + j], 0, 0))
    return pl.pallas_call(
        functools.partial(agent_kernel, head, listing),
        grid_spec=pltpu.PrefetchScalarGridSpec(
            num_scalar_prefetch=1,
            grid=(steps,),
            in_specs=[pl.BlockSpec(block, lambda t, p: (t, 0, 0))]
            + [pick(j) for j in range(listing)]
            + [whole(proj), whole(merge), whole(tproj)],
            out_specs=[
                pl.BlockSpec(block, lambda t, p: (t, 0, 0)),
                pl.BlockSpec((1, agents, 3 * width), lambda t, p: (t, 0, 0)),
            ],
        ),
        out_shape=[
            jax.ShapeDtypeStruct((steps, agents, width), jnp.float32),
            jax.ShapeDtypeStruct((steps, agents, 3 * width), jnp.bfloat16),
        ],
        compiler_params=pltpu.CompilerParams(vmem_limit_bytes=40 * 2**20),
        name="agent_attention",
    )(positions, embedded, *([arrived] * listing), proj, merge, tproj)


def time_kernel(head, res_ref, qkv_ref, prev_ref, merge_ref, weight_ref, out_ref, mix_ref):
    steps, agents, width = res_ref.shape
    coef = head**-0.5 * math.log2(math.e)
    oct_ = 8
    rows, cols = steps * oct_, 2 * steps * oct_
    r = lax.broadcasted_iota(jnp.int32, (rows, cols), 0)
    c = lax.broadcasted_iota(jnp.int32, (rows, cols), 1)
    qt, ks = r // oct_, c // oct_ - steps
    seen = (ks <= qt) & (ks > qt - WINDOW) & ((ks >= 0) | (lax.axis_index("tm") > 0))
    bias = jnp.where(seen & (r % oct_ == c % oct_), 0.0, NEG).astype(jnp.float32)
    bias = jnp.concatenate([bias, bias], axis=0)

    def halves(block):
        block = block.astype(jnp.float32)
        return [
            block[:, h : h + oct_].reshape(steps * oct_, block.shape[-1]).astype(jnp.bfloat16)
            for h in (0, oct_)
        ]

    def group(i, _):
        at = pl.ds(pl.multiple_of(i * 2 * oct_, 2 * oct_), 2 * oct_)
        for lo in range(0, width, 2 * head):
            hi = lo + 2 * head
            q = halves(qkv_ref[:, at, lo:hi])
            k0 = halves(prev_ref[:, at, lo:hi])
            k1 = halves(qkv_ref[:, at, width + lo : width + hi])
            v0 = halves(prev_ref[:, at, width + lo : width + hi])
            v1 = halves(qkv_ref[:, at, 2 * width + lo : 2 * width + hi])
            outs = []
            for h in range(2):
                k = jnp.concatenate([k0[h], k1[h]], axis=0)
                v = jnp.concatenate([v0[h], v1[h]], axis=0)
                o = pair_attention(q[h], k, v, head, coef, bias)
                outs.append(o.reshape(steps, oct_, hi - lo))
            mix_ref[:, at, lo:hi] = jnp.concatenate(outs, axis=1).astype(jnp.bfloat16)
        return 0

    lax.fori_loop(0, agents // (2 * oct_), group, 0)

    def finish(t, _):
        res = res_ref[t] + dot(mix_ref[t], merge_ref[...])
        square = res * res
        scaled = res * weight_ref[...]
        lanes = 128
        sq = sum(square[:, j : j + lanes] for j in range(0, width, lanes))
        sc = sum(scaled[:, j : j + lanes] for j in range(0, width, lanes))
        mean = jnp.sum(sq.T, axis=0, keepdims=True) / width
        out_ref[pl.ds(t, 1), :] = jnp.sum(sc.T, axis=0, keepdims=True) * lax.rsqrt(mean + epsilon)
        return 0

    lax.fori_loop(0, steps, finish, 0)


def time_call(res, qkv, prev, merge, weight, head):
    steps, agents, width = res.shape
    return pl.pallas_call(
        functools.partial(time_kernel, head),
        out_shape=jax.ShapeDtypeStruct((steps, agents), jnp.float32),
        in_specs=[pl.BlockSpec(memory_space=pltpu.VMEM)] * 5,
        out_specs=pl.BlockSpec(memory_space=pltpu.VMEM),
        scratch_shapes=[pltpu.VMEM((steps, agents, width), jnp.bfloat16)],
        compiler_params=pltpu.CompilerParams(vmem_limit_bytes=56 * 2**20),
        name="time_attention",
    )(res, qkv, prev, merge, weight.reshape(1, width))


def from_behind(value, axis, by):
    devices = lax.axis_size(axis)
    pairs = [(i, i + by) for i in range(devices) if 0 <= i + by < devices]
    return lax.ppermute(value, axis, pairs)


def advantage_pass(values, done_flags, rewards, bootstrap):
    steps = values.shape[0]
    parts = lax.axis_size("tm")
    last = lax.axis_index("tm") == parts - 1
    living = 1.0 - done_flags.astype(jnp.float32)
    factors = discount * trace_decay * living

    def run(following_last, running):
        following = jnp.concatenate([values[1:], following_last[None]], axis=0)
        changes = rewards + discount * living * following - values
        rows = [None] * steps
        for t in reversed(range(steps)):
            running = changes[t] + factors[t] * running
            rows[t] = running
        return jnp.stack(rows)

    zero = jnp.zeros_like(bootstrap)
    advantages = run(bootstrap, zero)
    for _ in range(parts - 1):
        sent = jnp.stack([values[0], advantages[0]])
        got = from_behind(sent, "tm", -1)
        advantages = run(jnp.where(last, bootstrap, got[0]), jnp.where(last, zero, got[1]))
    return advantages


def take_kernel(index, x_ref, out_ref):
    out_ref[...] = x_ref[...]


def take_steps(embedded, index):
    steps, agents, width = embedded.shape
    block = (1, agents, width)
    return pl.pallas_call(
        take_kernel,
        grid_spec=pltpu.PrefetchScalarGridSpec(
            num_scalar_prefetch=1,
            grid=index.shape,
            in_specs=[pl.BlockSpec(block, lambda i, p: (p[i], 0, 0))],
            out_specs=pl.BlockSpec(block, lambda i, p: (i, 0, 0)),
        ),
        out_shape=jax.ShapeDtypeStruct((index.shape[0], agents, width), embedded.dtype),
        name="take_steps",
    )(index, embedded)


def exchange(embedded, block_lists):
    steps, agents, width = embedded.shape
    listing = block_lists.shape[2]
    blocks = lax.axis_size("agent")
    capacity = max(2, (2 * steps * listing + blocks - 1) // blocks)
    peers = block_lists[0].reshape(-1)
    count = peers.shape[0]
    row_steps = jnp.arange(count, dtype=jnp.int32) // listing
    hits = (peers[:, None] == jnp.arange(blocks, dtype=jnp.int32)[None, :]).astype(jnp.int32)
    order = jnp.arange(count, dtype=jnp.int32)
    before = (order[None, :] < order[:, None]).astype(jnp.int32)
    earlier = jnp.sum(before[:, :, None] * hits[None], axis=1)
    slot = jnp.sum(earlier * hits, axis=1)
    slots = (slot[:, None] == jnp.arange(capacity, dtype=jnp.int32)[None, :]).astype(jnp.int32)
    requests = jnp.sum((hits * row_steps[:, None])[:, :, None] * slots[:, None, :], axis=0)
    wanted = lax.all_to_all(requests, "agent", split_axis=0, concat_axis=0, tiled=True)
    outgoing = take_steps(embedded, wanted.reshape(-1)).reshape(blocks, capacity, agents, width)
    arrived = lax.all_to_all(outgoing, "agent", split_axis=0, concat_axis=0, tiled=True)
    return arrived.reshape(blocks * capacity, agents, width), peers * capacity + slot


OCT = 8
SHARES = (2, 4, 4, 4, 2)


def parts_of(agents):
    unit, parts, start = agents // sum(SHARES), [], 0
    for share in SHARES:
        parts.append((start, share * unit))
        start += share * unit
    return parts


def partner(me, k, count):
    other, bit = 0, 1
    while bit < count:
        a, b = lax.rem(lax.div(me, bit), 2), lax.rem(lax.div(k, bit), 2)
        other = other + bit * (a + b - 2 * a * b)
        bit *= 2
    return other


def weighted(e, v, first):
    rows, wide = first.shape
    both = dot(e, jnp.concatenate([v, jnp.ones_like(v)], axis=1))
    o = both[:, :wide] / both[:, wide:]
    return jnp.where(first, o[:rows], o[rows:])


def heads_attention(q, k, v, head):
    rows = q.shape[0]
    first = lax.broadcasted_iota(jnp.int32, q.shape, 1) < head
    zero = jnp.zeros_like(q)
    both = jnp.concatenate([jnp.where(first, q, zero), jnp.where(first, zero, q)], axis=0)
    s = lax.dot_general(both, k, (((1,), (1,)), ((), ())), preferred_element_type=jnp.float32)
    e = jnp.exp2(s - jnp.max(s, axis=-1, keepdims=True))
    return weighted(e.astype(jnp.bfloat16), v, first)


def step_split_kernel(
    head, x_in, lists_ref, proj_in, merge_in, tproj_in, tmerge_in, weight_in, done_in, reward_in,
    boot_in, out_ref,
    x_ref, proj, merge, tproj, tmerge, weight_ref, done_ref, reward_ref, boot_ref,
    lists_in, lists, arrived, qkv, stage, ret, res_ref, q_ref, kv_ref, prev_ref, mix_ref, sum_ref,
    own_ref, edge_out, edge_in,
    list_send, list_recv, go_send, go_recv, back_send, back_recv, part_send, part_recv,
    kv_send, kv_recv, kvp_send, kvp_recv, list_sem, edge_sem, load_sem,
):
    values_ref, adv_ref = out_ref.at[0], out_ref.at[1]
    steps, agents, width = x_in.shape
    listing = lists_ref.shape[0]
    blocks = lax.axis_size("agent")
    phases = steps // blocks
    me, tm = lax.axis_index("agent"), lax.axis_index("tm")
    earlier, later = tm > 0, tm < lax.axis_size("tm") - 1
    parts = parts_of(agents)
    last, final = phases - 1, len(parts) - 1
    oct_ = OCT
    coef = head**-0.5 * math.log2(math.e)

    barrier = pltpu.get_barrier_semaphore()

    def greet(k, _):
        peer = {"agent": partner(me, k, blocks)}
        pl.semaphore_signal(barrier, inc=1, device_id=peer, device_id_type=MESH)
        return 0

    lax.fori_loop(1, blocks, greet, 0)

    @pl.when(earlier)
    def _():
        pl.semaphore_signal(barrier, inc=1, device_id={"tm": tm - 1}, device_id_type=MESH)

    @pl.when(later)
    def _():
        pl.semaphore_signal(barrier, inc=1, device_id={"tm": tm + 1}, device_id_type=MESH)

    pl.semaphore_wait(barrier, blocks - 1 + earlier.astype(jnp.int32) + later.astype(jnp.int32))

    def remote(src, dst, send, recv, device):
        return pltpu.make_async_remote_copy(
            src_ref=src, dst_ref=dst, send_sem=send, recv_sem=recv,
            device_id=device, device_id_type=MESH,
        )

    def list_copy(k):
        peer = {"agent": partner(me, k, blocks)}
        return remote(lists_ref, lists_in.at[me], list_send.at[k], list_recv.at[k], peer)

    def go_copy(p, k):
        other = partner(me, k, blocks)
        return remote(
            x_in.at[p * blocks + other], arrived.at[p, me], go_send.at[p, k], go_recv.at[p, k],
            {"agent": other},
        )

    def back_copy(p, k):
        other = partner(me, k, blocks)
        return remote(
            stage.at[p, other], ret.at[p * blocks + me], back_send.at[p, k], back_recv.at[p, k],
            {"agent": other},
        )

    def part_copy(j, k):
        other = partner(me, k, blocks)
        at = pl.ds(*parts[j])
        return remote(
            stage.at[last, other, at], ret.at[last * blocks + me, at], part_send.at[j, k],
            part_recv.at[j, k], {"agent": other},
        )

    count = lax.axis_size("tm")
    after, before = {"tm": lax.rem(tm + 1, count)}, {"tm": lax.rem(tm + count - 1, count)}
    pairs = last * blocks // 2

    def kv_copy(i):
        at = pl.ds(pl.multiple_of(i * 2 * oct_, 2 * oct_), 2 * oct_)
        return remote(kv_ref.at[:, at], prev_ref.at[:, at], kv_send.at[i], kv_recv.at[i], after)

    def kv_part_copy(j):
        start, size = parts[j]
        at, rows = pl.ds(start // oct_, size // oct_), pl.ds(last * blocks * oct_, blocks * oct_)
        return remote(
            kv_ref.at[at, rows], prev_ref.at[at, rows], kvp_send.at[j], kvp_recv.at[j], after
        )

    def edge_copy():
        return remote(edge_out, edge_in, edge_sem.at[0], edge_sem.at[1], before)

    def send_lists(k, _):
        list_copy(k).start()
        return 0

    lax.fori_loop(1, blocks, send_lists, 0)

    def send_out(i, _):
        p, k = lax.div(i, blocks), lax.rem(i, blocks)

        @pl.when(k > 0)
        def _():
            go_copy(p, k).start()

        return 0

    lax.fori_loop(0, phases * blocks, send_out, 0)

    mine = [
        pltpu.make_async_copy(x_in.at[p * blocks + me], arrived.at[p, me], load_sem.at[p])
        for p in range(phases)
    ]
    outside = [proj_in, merge_in, tproj_in, tmerge_in, x_in, weight_in, done_in, reward_in, boot_in]
    inside = [proj, merge, tproj, tmerge, x_ref, weight_ref, done_ref, reward_ref, boot_ref]
    loads = [
        pltpu.make_async_copy(a, b, load_sem.at[phases + i])
        for i, (a, b) in enumerate(zip(outside, inside))
    ]
    for load in mine + loads:
        load.start()
    lists_in[me] = lists_ref[...]

    @pl.when(jnp.logical_not(earlier))
    def _():
        def clear(o, _):
            prev_ref[o] = jnp.zeros(prev_ref.shape[1:], prev_ref.dtype)
            return 0

        lax.fori_loop(0, prev_ref.shape[0], clear, 0)

    def got_list(k, _):
        list_copy(k).wait_recv()
        return 0

    lax.fori_loop(1, blocks, got_list, 0)
    to_scalars = pltpu.make_async_copy(lists_in, lists, list_sem)
    to_scalars.start()
    to_scalars.wait()

    for load in mine + loads[:1]:
        load.wait()

    def project(p):
        def pair(i, _):
            @pl.when(i > 0)
            def _():
                go_copy(p, 2 * i).wait_recv()

            go_copy(p, 2 * i + 1).wait_recv()
            low = 2 * lax.div(partner(me, 2 * i, blocks), 2)
            x = arrived[p, pl.ds(low, 2)].reshape(2 * agents, width)
            normed = normed_bf16(x.astype(jnp.float32))
            for c in range(3):
                cols = slice(c * width, (c + 1) * width)
                y = dot(normed, proj[:, cols])
                if c == 0:
                    y = y * coef
                qkv[pl.ds(low, 2), :, cols] = y.astype(jnp.bfloat16).reshape(2, agents, width)
            return 0

        lax.fori_loop(0, blocks // 2, pair, 0)

    def attend(p, b):
        chosen = [lists[b, j, p * blocks + me] for j in range(listing)]
        outs = []
        for lo in range(0, width, 2 * head):
            hi = lo + 2 * head

            def keys(offset):
                rows = [qkv[b, :, offset + lo : offset + hi]]
                rows += [qkv[i, :, offset + lo : offset + hi] for i in chosen]
                return jnp.concatenate(rows, axis=0)

            q = qkv[b, :, lo:hi]
            outs.append(heads_attention(q, keys(width), keys(2 * width), head))
        return jnp.concatenate(outs, axis=1).astype(jnp.bfloat16)

    for p in range(phases):
        project(p)

        def answer(i, _, p=p):
            k = blocks - 1 - i
            b = partner(me, k, blocks)
            stage[p, b] = attend(p, b)

            @pl.when(k > 0)
            def _():
                if p < last:
                    back_copy(p, k).start()
                else:
                    part_copy(0, k).start()

            return 0

        lax.fori_loop(0, blocks, answer, 0)
        ret[p * blocks + me] = stage[p, me]

    ahead = 2

    def send_part(j):
        def one(i, _):
            part_copy(j, blocks - 1 - i).start()
            return 0

        lax.fori_loop(0, blocks - 1, one, 0)

    for j in range(1, min(ahead, final + 1)):
        send_part(j)

    for load in loads[1:]:
        load.wait()

    def layer(x, mixed, put_res, put_q, put_kv, send):
        res = x.astype(jnp.float32) + dot(mixed, merge[...])
        put_res(res)
        normed = normed_bf16(res)
        put_kv(0, dot(normed, tproj[:, width : 2 * width]))
        put_kv(1, dot(normed, tproj[:, 2 * width :]))
        pl.when(later)(send)
        put_q(dot(normed, tproj[:, :width]) * coef)

    def by_oct(value, parts, group):
        rows = value.reshape(parts, group, oct_, value.shape[-1])
        return [
            jnp.concatenate([rows[t, o] for t in range(parts)], axis=0) for o in range(group)
        ]

    def early(n, _):
        p, i = lax.div(n, blocks // 2), lax.rem(n, blocks // 2)

        @pl.when(i > 0)
        def _():
            back_copy(p, 2 * i).wait_recv()

        back_copy(p, 2 * i + 1).wait_recv()
        low = p * blocks + 2 * lax.div(partner(me, 2 * i, blocks), 2)
        at = pl.ds(pl.multiple_of(low * oct_, 2 * oct_), 2 * oct_)

        def put(ref, cols):
            def store(value):
                for o, rows in enumerate(by_oct(value, 2, agents // oct_)):
                    ref[o, at, cols] = rows.astype(ref.dtype)

            return store

        def put_kv(c, value):
            put(kv_ref, slice(c * width, (c + 1) * width))(value)

        layer(
            x_ref[pl.ds(low, 2)].reshape(2 * agents, width),
            ret[pl.ds(low, 2)].reshape(2 * agents, width),
            put(res_ref, slice(0, width)), put(q_ref, slice(0, width)), put_kv,
            lambda: kv_copy(lax.div(low, 2)).start(),
        )

        return 0

    lax.fori_loop(0, pairs, early, 0)

    @pl.when(earlier)
    def _():
        def ready(i, _):
            kv_copy(i).wait_recv()
            return 0

        lax.fori_loop(0, pairs, ready, 0)

    rows = steps * oct_
    qt = lax.broadcasted_iota(jnp.int32, (2 * rows, rows), 0)
    ks = lax.broadcasted_iota(jnp.int32, (2 * rows, rows), 1)
    same = lax.rem(qt, oct_) == lax.rem(ks, oct_)
    own = lax.div(ks, oct_) <= lax.div(lax.rem(qt, rows), oct_)
    bias = jnp.where(same & (own | earlier), 0.0, NEG).astype(jnp.float32)
    own_ref[...] = jnp.where(own, 1.0, 0.0).astype(jnp.float32).astype(jnp.bfloat16)
    lanes = 128
    first = lax.broadcasted_iota(jnp.int32, (rows, 2 * head), 1) < head

    def time_oct(o, slot):
        q = q_ref[o]
        for lo in range(0, width, 2 * head):
            hi = lo + 2 * head
            piece = q[:, lo:hi]
            zero = jnp.zeros_like(piece)
            both = jnp.concatenate(
                [jnp.where(first, piece, zero), jnp.where(first, zero, piece)], axis=0
            )
            k = jnp.concatenate([kv_ref[o, :, lo:hi], prev_ref[o, :, lo:hi]], axis=0)
            v = jnp.concatenate(
                [kv_ref[o, :, width + lo : width + hi], prev_ref[o, :, width + lo : width + hi]],
                axis=0,
            )
            s = lax.dot_general(
                both, k, (((1,), (1,)), ((), ())), preferred_element_type=jnp.float32
            )
            s = jnp.where(own, s[:, :rows], s[:, rows:]) + bias
            e = jnp.exp2(s - jnp.max(s, axis=-1, keepdims=True)).astype(jnp.bfloat16)
            here = e * own_ref[...]
            out = weighted(jnp.concatenate([here, e - here], axis=1), v, first)
            mix_ref[slot * rows : (slot + 1) * rows, lo:hi] = out.astype(jnp.bfloat16)

    def front(j):
        start, size = parts[j]
        octs = size // oct_

        def here(k, _):
            part_copy(j, k).wait_recv()
            return 0

        lax.fori_loop(1, blocks, here, 0)
        at = pl.ds(start, size)
        turn = slice(last * blocks, steps)
        late = slice(last * blocks * oct_, rows)

        def put(ref, cols):
            def store(value):
                for o, piece in enumerate(by_oct(value, blocks, octs)):
                    ref[start // oct_ + o, late, cols] = piece.astype(ref.dtype)

            return store

        def put_kv(c, value):
            put(kv_ref, slice(c * width, (c + 1) * width))(value)

        layer(
            x_ref[turn, at].reshape(blocks * size, width),
            ret[turn, at].reshape(blocks * size, width),
            put(res_ref, slice(0, width)), put(q_ref, slice(0, width)), put_kv,
            lambda: kv_part_copy(j).start(),
        )

    lane = lax.broadcasted_iota(jnp.int32, (1, lanes), 1)

    def back(j):
        start, size = parts[j]
        octs = size // oct_

        @pl.when(earlier)
        def _():
            kv_part_copy(j).wait_recv()

        for o in range(octs):
            time_oct(start // oct_ + o, o)
        used = slice(0, octs * rows)
        sum_ref[used] = dot(mix_ref[used], tmerge[...])
        per = lanes // size
        inside = (lane >= start) & (lane < start + size)
        for i in range(steps // per):
            squares, scales = [], []
            for r in range(per):
                for o in range(octs):
                    spot = slice((i * per + r) * oct_, (i * per + r + 1) * oct_)
                    wide = slice(o * rows + spot.start, o * rows + spot.stop)
                    res = res_ref[start // oct_ + o, spot] + sum_ref[wide]
                    square, scaled = res * res, res * weight_ref[...]
                    squares.append(sum(square[:, lo : lo + lanes] for lo in range(0, width, lanes)))
                    scales.append(sum(scaled[:, lo : lo + lanes] for lo in range(0, width, lanes)))
            square, scaled = jnp.concatenate(squares, axis=0), jnp.concatenate(scales, axis=0)
            mean = jnp.sum(square.T, axis=0, keepdims=True) / width
            value = jnp.sum(scaled.T, axis=0, keepdims=True) * lax.rsqrt(mean + epsilon)
            value = jnp.broadcast_to(value, (oct_, lanes))
            for r in range(per):
                shift = (start - r * size) % lanes
                turned = pltpu.roll(value, shift, 1) if shift else value
                t = i * per + r
                if j > 0:
                    kept = values_ref[t : t + 1, :]
                    values_ref[t : t + 1, :] = jnp.where(inside, turned[:1], kept)
                else:
                    values_ref[t : t + 1, :] = turned[:1]

    for j in range(final + 1):
        if j == final:
            back(j - 1)
        front(j)
        if j + ahead <= final:

            def gone(k, _, j=j):
                part_copy(j, k).wait_send()
                return 0

            lax.fori_loop(1, blocks, gone, 0)
            send_part(j + ahead)
        if 0 < j < final:
            back(j - 1)
    back(final)

    running, gain = jnp.zeros((1, agents), jnp.float32), jnp.ones((1, agents), jnp.float32)
    found, gains = [], []
    following = jnp.zeros((1, agents), jnp.float32)
    for t in reversed(range(steps)):
        living = 1.0 - done_ref[t : t + 1, :].astype(jnp.float32)
        value = values_ref[t : t + 1, :]
        change = reward_ref[t : t + 1, :] + discount * living * following - value
        running = change + discount * trace_decay * living * running
        gain = gain * (discount * living if t == steps - 1 else discount * trace_decay * living)
        following = value
        found.append(running)
        gains.append(gain)

    @pl.when(later)
    def _():
        edge_copy().wait_recv()
        edge_out[...] = edge_in[...]

    @pl.when(jnp.logical_not(later))
    def _():
        edge_out[0:1, :] = boot_ref[...]
        edge_out[1:2, :] = jnp.zeros_like(boot_ref)

    beyond = edge_out[0:1, :] + trace_decay * edge_out[1:2, :]
    edge_out[0:1, :] = value
    edge_out[1:2, :] = running + gain * beyond

    @pl.when(earlier)
    def _():
        edge_copy().start()

    for t in range(steps):
        adv_ref[t : t + 1, :] = found[steps - 1 - t] + gains[steps - 1 - t] * beyond

    def drain(k, _):
        list_copy(k).wait_send()
        for p in range(phases):
            go_copy(p, k).wait_send()
            if p < last:
                back_copy(p, k).wait_send()
        for j in range(max(0, final + 1 - ahead), final + 1):
            part_copy(j, k).wait_send()
        return 0

    lax.fori_loop(1, blocks, drain, 0)

    @pl.when(later)
    def _():
        def gone(i, _):
            kv_copy(i).wait_send()
            return 0

        lax.fori_loop(0, pairs, gone, 0)

        for j in range(final + 1):
            kv_part_copy(j).wait_send()

    @pl.when(earlier)
    def _():
        edge_copy().wait_send()


def step_split_call(
    embedded, lists, proj, merge, tproj, tmerge, weight, done, rewards, bootstrap, head
):
    steps, agents, width = embedded.shape
    listing = lists.shape[0]
    blocks = lax.axis_size("agent")
    phases = steps // blocks
    parts = len(SHARES)
    size = max(part[1] for part in parts_of(agents))
    vmem, hbm = pl.BlockSpec(memory_space=pltpu.VMEM), pl.BlockSpec(memory_space=pl.ANY)
    dma = pltpu.SemaphoreType.DMA
    out = jax.ShapeDtypeStruct((2, steps, agents), jnp.float32)
    b16, f32 = jnp.bfloat16, jnp.float32
    pairs = max(1, (phases - 1) * blocks // 2)
    return pl.pallas_call(
        functools.partial(step_split_kernel, head),
        in_specs=[hbm, vmem] + [hbm] * 8,
        out_specs=vmem,
        out_shape=out,
        scratch_shapes=[
            pltpu.VMEM((steps, agents, width), b16),
            pltpu.VMEM((width, 3 * width), b16),
            pltpu.VMEM((width, width), b16),
            pltpu.VMEM((width, 3 * width), b16),
            pltpu.VMEM((width, width), b16),
            pltpu.VMEM((1, width), f32),
            pltpu.VMEM((steps, agents), jnp.int32),
            pltpu.VMEM((steps, agents), f32),
            pltpu.VMEM((1, agents), f32),
            pltpu.VMEM((blocks, listing, steps), jnp.int32),
            pltpu.SMEM((blocks, listing, steps), jnp.int32),
            pltpu.VMEM((phases, blocks, agents, width), b16),
            pltpu.VMEM((blocks, agents, 3 * width), b16),
            pltpu.VMEM((phases, blocks, agents, width), b16),
            pltpu.VMEM((steps, agents, width), b16),
            pltpu.VMEM((agents // 8, steps * 8, width), f32),
            pltpu.VMEM((agents // 8, steps * 8, width), b16),
            pltpu.VMEM((agents // 8, steps * 8, 2 * width), b16),
            pltpu.VMEM((agents // 8, steps * 8, 2 * width), b16),
            pltpu.VMEM((size * steps, width), b16),
            pltpu.VMEM((size * steps, width), f32),
            pltpu.VMEM((2 * 8 * steps, 8 * steps), b16),
            pltpu.VMEM((2, agents), f32),
            pltpu.VMEM((2, agents), f32),
            dma((blocks,)), dma((blocks,)),
            dma((phases, blocks)), dma((phases, blocks)),
            dma((phases, blocks)), dma((phases, blocks)),
            dma((parts, blocks)), dma((parts, blocks)),
            dma((pairs,)), dma((pairs,)),
            dma((parts,)), dma((parts,)),
            dma(()), dma((2,)), dma((phases + 9,)),
        ],
        compiler_params=pltpu.CompilerParams(
            collective_id=0, has_side_effects=True, vmem_limit_bytes=58 * 2**20
        ),
        name="critic_layer",
    )(
        embedded, lists, proj, merge, tproj, tmerge, weight.reshape(1, width),
        done, rewards, bootstrap.reshape(1, agents),
    )


def body(
    embedded,
    block_lists,
    done_flags,
    rewards,
    bootstrap,
    agent_proj,
    agent_merge,
    time_proj,
    time_merge,
    value_weight,
):
    steps, agents, width = embedded.shape
    head = width // HEADS
    assert steps == WINDOW
    blocks = lax.axis_size("agent")
    if steps % blocks == 0 and blocks & (blocks - 1) == 0 and blocks > 1 and agents == 128:
        both = (
            step_split_call(
                embedded, block_lists[0].T, agent_proj, agent_merge, time_proj, time_merge,
                value_weight, done_flags, rewards, bootstrap, head,
            )
        )
        return both[0], both[1]
    arrived, positions = exchange(embedded, block_lists)
    res, qkv = agent_call(embedded, arrived, positions, agent_proj, agent_merge, time_proj, head)
    prev = from_behind(qkv[:, :, width:], "tm", 1)
    values = time_call(res, qkv, prev, time_merge, value_weight, head)
    return (values, advantage_pass(values, done_flags, rewards, bootstrap))


def solution(mesh):
    placed = (
        P(("groups", "tm"), "agent", None),
        P(("groups", "agent"), "tm", None),
        P(("groups", "tm"), "agent"),
        P(("groups", "tm"), "agent"),
        P(("groups", "agent")),
        P(),
        P(),
        P(),
        P(),
        P(),
    )
    return jax.shard_map(
        body,
        mesh=mesh,
        in_specs=placed,
        out_specs=(P(("groups", "tm"), "agent"), P(("groups", "tm"), "agent")),
        check_vma=False,
    )
```
